32 devices in a mesh: gx: 4 (over x, core), gy: 8 (over z, y).
Axes of the slice: x: 2, y: 2, z: 4, core: 2. Of those that a mesh axis runs over, the one named last changes fastest.
Arguments:
- adjoint: float32 [2, 256, 768, 128], P(None, 'gx', 'gy'), may hold values from -6 to 6
- medium: bfloat16 [5, 256, 768, 128], P(None, 'gx', 'gy'), may hold values from -4 to 4, as said below
- rotors: float32 [4, 2048], P(None, ('gx', 'gy')), may hold values from -0.5 to 2
- step_size: float32 [], replicated, may hold values from 0.02 to 0.1
- slot_turbine: int32 [6144], P(('gx', 'gy')), may hold values from -1 to 2047, as said below
- slot_corner: int32 [3, 6144], P(None, ('gx', 'gy')), may hold values from 0 to 112, as said below
- moved_rotors: int32 [128], P(('gx', 'gy')), may hold values from 0 to 63, as said below
- new_brick: int32 [128, 1], P(('gx', 'gy')), may hold values from 0 to 31; in each aligned block of 128 rows (0 to 127, 128 to 255, ...) at most 8 rows name the same one
Outputs:
- adjoint_out: float32 [2, 256, 768, 128], P(None, 'gx', 'gy')
- step_taken: float32 [2, 2048], P(None, ('gx', 'gy'))
- incoming: bfloat16 [256, 2048], P(('gx', 'gy'))
The draws below stay inside these ranges and needn't reach their ends.
Inputs may be any that keep to these rules, and one draw needn't show every extreme that they name: `slot_turbine`: entries are global turbine numbers or -1 for an empty slot. Every turbine is listed exactly once over all bricks. A brick lists at most 192 turbines, and some brick lists exactly 192. `slot_corner`: every listed block of 8 x 16 x 16 cells lies inside its brick. `moved_rotors`: the 4 entries of one owner are distinct. `new_brick`: over all moved rotors, no brick is named more than 8 times, a bound that some block reaches. `medium`: viscosity in 0.1 to 1, velocity in 0.2 to 1, dissipation in 0.1 to 1, coupling in -0.3 to 0.3, source in -4 to 4.
All inputs are finite; a program needn't handle non-finite values.
Results may differ from the reference program's by a relative error of at most 0.001.
Values may be sent and summed in bfloat16 or wider, within the bound.
A program may use at most 256 MiB of HBM per device.

```python
import math
import jax
import jax.numpy as jnp
import numpy as np
from jax import lax

CX = 64
CY = 96
CZ = 128
TURB_DEV = 64
MOVED_DEV = 4
KX = 8
KY = 16
KZ = 16
SWEEPS = 2
RECV = 8
BRICKS = 32
NX = 256
NY = 768
NZ = 128
TURBINES = 2048
SLOTS = 192
MOVED = 128
N_GX = 4
N_GY = 8


def loguniform_field(key, shape, low, high):
    return jnp.exp(jax.random.uniform(key, shape, jnp.float32, math.log(low), math.log(high)))


def draw_medium(key, part):
    shape = (NX, NY, NZ)
    keys = [jax.random.fold_in(key, 100 + index) for index in range(5)]
    viscous = loguniform_field(keys[0], shape, 0.1, 1.0)
    velocity = jax.random.uniform(keys[1], shape, jnp.float32, 0.2, 1.0)
    reaction = loguniform_field(keys[2], shape, 0.1, 1.0)
    coupling = jax.random.uniform(keys[3], shape, jnp.float32, -0.3, 0.3)
    source = jnp.clip(jax.random.normal(keys[4], shape, jnp.float32), -4.0, 4.0)
    return jnp.stack([viscous, velocity, reaction, coupling, source]).astype(jnp.bfloat16)


def draw_rotors(key, part):
    keys = [jax.random.fold_in(key, 200 + index) for index in range(4)]
    shape = (TURBINES,)
    offset_x = jax.random.uniform(keys[0], shape, jnp.float32, -0.5, 0.5)
    offset_y = jax.random.uniform(keys[1], shape, jnp.float32, -0.5, 0.5)
    yaw_angle = jax.random.uniform(keys[2], shape, jnp.float32, -0.5, 0.5)
    thrust = loguniform_field(keys[3], shape, 0.5, 2.0)
    return jnp.stack([offset_x, offset_y, yaw_angle, thrust])


def draw_slot_turbine(key, part):
    key_rank = jax.random.fold_in(key, 11)
    key_ids = jax.random.fold_in(key, 12)
    ordering = jax.random.permutation(key_rank, BRICKS)
    rank_of = jnp.zeros((BRICKS,), jnp.int32).at[ordering].set(jnp.arange(BRICKS, dtype=jnp.int32))
    counts = jnp.where(rank_of < BRICKS // 4, 3 * TURB_DEV, jnp.where(rank_of < BRICKS // 2, TURB_DEV, 0)).astype(jnp.int32)
    starts = jnp.cumsum(counts) - counts
    slot_number = jnp.arange(SLOTS, dtype=jnp.int32)
    filled = slot_number[None, :] < counts[:, None]
    flat_index = jnp.clip(starts[:, None] + slot_number[None, :], 0, TURBINES - 1)
    numbers = jax.random.permutation(key_ids, TURBINES).astype(jnp.int32)
    table = jnp.where(filled, numbers[flat_index], -1)
    return table.reshape(BRICKS * SLOTS).astype(jnp.int32)


def draw_slot_corner(key, part):
    shape = (BRICKS * SLOTS,)
    corner_x = jax.random.randint(jax.random.fold_in(key, 21), shape, 0, CX - KX + 1)
    corner_y = jax.random.randint(jax.random.fold_in(key, 22), shape, 0, CY - KY + 1)
    corner_z = jax.random.randint(jax.random.fold_in(key, 23), shape, 0, CZ - KZ + 1)
    return jnp.stack([corner_x, corner_y, corner_z]).astype(jnp.int32)


def draw_moved_rotors(key, part):
    keys = jax.random.split(jax.random.fold_in(key, 300), BRICKS)

    def choose_some(owner_key):
        return jax.random.permutation(owner_key, TURB_DEV)[:MOVED_DEV]
    return jax.vmap(choose_some)(keys).reshape(MOVED).astype(jnp.int32)


def level_of(own_key, dims, cuts, low, high):
    def one(dim, parts):
        steps = jax.random.uniform(jax.random.fold_in(jax.random.fold_in(own_key, 6), dim), (parts,), jnp.float32, low / len(cuts), high / len(cuts))
        return jnp.repeat(jnp.exp(steps), dims[dim] // parts).reshape((-1,) + (1,) * (len(dims) - dim - 1))

    gain = one(*cuts[0])
    for cut in cuts[1:]:
        gain = gain * one(*cut)
    return gain


def deal_out(key, own, number, rows, number_of, top, most, skew):
    ranking = jax.random.permutation(key, number_of)
    crowded, usual = load_shares(number_of, rows * top, most, skew, True), load_shares(number_of, rows * top, most, skew, False)
    places = jnp.arange(number_of)

    def named(sizes, offset_by):
        used = int((sizes > 0).sum())
        fixed = max(1, used // 4)
        moved = fixed + (places - fixed + offset_by * (used - fixed)) % max(1, number_of - fixed)
        return jnp.zeros((number_of,), jnp.int32).at[ranking[jnp.where(places < fixed, places, moved)]].set(jnp.asarray(sizes, jnp.int32))

    sizes = jnp.where(number % 4 == 0, named(crowded, number // 4), named(usual, number - number // 4 - 1))
    mixed = jax.random.permutation(jax.random.fold_in(own, 3), number_of)
    giver, taker = mixed[0:number_of // 2 * 2:2], mixed[1:number_of // 2 * 2:2]
    margin = jnp.minimum(sizes[giver] - 1, most - sizes[taker]) // 2
    margin = jnp.where((giver == ranking[0]) | (taker == ranking[0]) | (sizes[taker] == 0), 0, jnp.maximum(margin, 0))
    moved = jax.random.randint(jax.random.fold_in(own, 4), (number_of // 2,), 0, 1 << 20) % (margin + 1)
    sizes = sizes.at[giver].add(-moved).at[taker].add(moved)
    labels = jnp.searchsorted(jnp.cumsum(sizes), jnp.arange(rows * top), side="right").astype(jnp.int32)
    listing = labels.reshape(top, rows).T
    listing = listing[jax.random.permutation(jax.random.fold_in(own, 1), rows)]
    offset_by = jax.random.randint(jax.random.fold_in(own, 2), (rows, 1), 0, top)
    return jnp.take_along_axis(listing, (jnp.arange(top)[None, :] + offset_by) % top, axis=1)


def load_shares(number_of, total, most, slope, full):
    loads = [(1 << 20) // math.isqrt(standing ** slope) + 1 for standing in range(1, number_of + 1)]
    largest = most if full else min(most, max(-(-total // number_of), total * loads[0] // sum(loads)))
    least = 1 if total - largest >= number_of - 1 else 0
    given, surplus = [largest] + [least] * (number_of - 1), total - largest - least * (number_of - 1)
    while surplus > 0:
        movable = [i for i in range(1, number_of) if given[i] < largest] or [i for i in range(1, number_of) if given[i] < most]
        pool, left = sum([loads[i] for i in movable]), surplus
        for i in movable:
            addition = min(most - given[i], max(1, left * loads[i] // pool), surplus)
            given[i] = given[i] + addition
            surplus = surplus - addition
    return np.array(given)


def noise(key, dims, scale, limit, cuts=(), kind=jnp.bfloat16):
    gain = level_of(key, dims, cuts, -0.22, 0.18) if cuts else 1.0
    values = jax.random.normal(key, dims, jnp.float32) * scale * gain
    return jnp.minimum(jnp.maximum(values, -limit), limit).astype(kind)


def setup_inputs(seed: int = 0) -> dict:
    seeds = jax.random.split(jax.random.key(seed), 9)
    adjoint = noise(seeds[0], (2, NX, NY, NZ), 1.0, 6.0, ((1, 4), (2, 8)), jnp.float32)
    medium = draw_medium(jax.random.fold_in(seeds[8], 71), 0)
    rotors = draw_rotors(jax.random.fold_in(seeds[8], 71), 0)
    step_size = jnp.clip(jnp.exp(jax.random.uniform(seeds[3], (), jnp.float32, math.log(0.02), math.log(0.1))), 0.02, 0.1)
    slot_turbine = draw_slot_turbine(jax.random.fold_in(seeds[8], 71), 0)
    slot_corner = draw_slot_corner(jax.random.fold_in(seeds[8], 71), 0)
    moved_rotors = draw_moved_rotors(jax.random.fold_in(seeds[8], 71), 0)
    new_brick_keys = jax.random.split(jax.random.fold_in(seeds[7], 1), MOVED // MOVED)
    new_brick_turns = jax.random.permutation(jax.random.fold_in(seeds[7], 3), MOVED // MOVED)
    new_brick = jax.vmap(lambda own, number: deal_out(jax.random.fold_in(seeds[7], 2), own, number, MOVED, BRICKS, 1, RECV, 2))(new_brick_keys, new_brick_turns).reshape((MOVED, 1))
    return {"adjoint": adjoint, "medium": medium, "rotors": rotors, "step_size": step_size, "slot_turbine": slot_turbine, "slot_corner": slot_corner, "moved_rotors": moved_rotors, "new_brick": new_brick}


TAU = 0.05
SIGMA_AXIAL = 1.5
SIGMA_RADIAL = 4.0


def relax_cells(padded, viscous, velocity, reaction, coupling, source):
    fluxes = viscous[None] * padded
    side_sum = fluxes[:, 2:, 1:-1] + fluxes[:, :-2, 1:-1] + fluxes[:, 1:-1, 2:] + fluxes[:, 1:-1, :-2]
    centre = padded[:, 1:-1, 1:-1]
    inner_flux = fluxes[:, 1:-1, 1:-1]
    zero_layer = jnp.zeros_like(inner_flux[..., :1])
    vertical = jnp.concatenate([inner_flux[..., 1:], zero_layer], axis=-1) + jnp.concatenate([zero_layer, inner_flux[..., :-1]], axis=-1)
    carried = velocity[None, 2:, 1:-1] * padded[:, 2:, 1:-1]
    diagonal = 6.0 * viscous[1:-1, 1:-1] + velocity[1:-1, 1:-1] + reaction
    image_k = diagonal * centre[0] + coupling * centre[1] - side_sum[0] - vertical[0] - carried[0]
    image_e = (diagonal + reaction) * centre[1] + coupling * centre[0] - side_sum[1] - vertical[1] - carried[1]
    return jnp.stack([centre[0] + TAU * (source - image_k), centre[1] - TAU * image_e])


def disk_shape(sub_x, sub_y, yaw_angle, thrust):
    axis_x = jnp.arange(KX).astype(jnp.float32) + 0.5 - KX / 2.0
    axis_y = jnp.arange(KY).astype(jnp.float32) + 0.5 - KY / 2.0
    axis_z = jnp.arange(KZ).astype(jnp.float32) + 0.5 - KZ / 2.0
    delta_x = axis_x[None, :, None, None] - sub_x[:, None, None, None]
    delta_y = axis_y[None, None, :, None] - sub_y[:, None, None, None]
    height = axis_z[None, None, None, :]
    cosine = jnp.cos(yaw_angle)[:, None, None, None]
    sine_yaw = jnp.sin(yaw_angle)[:, None, None, None]
    along_axis = cosine * delta_x + sine_yaw * delta_y
    across = cosine * delta_y - sine_yaw * delta_x
    kernel = thrust[:, None, None, None] * jnp.exp(-along_axis * along_axis / (2.0 * SIGMA_AXIAL * SIGMA_AXIAL) - (across * across + height * height) / (2.0 * SIGMA_RADIAL * SIGMA_RADIAL))
    return kernel, along_axis, across, cosine, sine_yaw


def disk_slopes(blocks, sub_x, sub_y, yaw_angle, thrust):
    kernel, along_axis, across, cosine, sine_yaw = disk_shape(sub_x, sub_y, yaw_angle, thrust)
    axial_part = along_axis / (SIGMA_AXIAL * SIGMA_AXIAL)
    radial_part = across / (SIGMA_RADIAL * SIGMA_RADIAL)
    slope_x = kernel * (axial_part * cosine - radial_part * sine_yaw)
    slope_y = kernel * (axial_part * sine_yaw + radial_part * cosine)
    return jnp.stack([jnp.sum(blocks * slope_x, axis=(1, 2, 3)), jnp.sum(blocks * slope_y, axis=(1, 2, 3))])


def reference(adjoint, medium, rotors, step_size, slot_turbine, slot_corner, moved_rotors, new_brick):
    coefficients = medium.astype(jnp.float32)
    plane_pad = ((1, 1), (1, 1), (0, 0))
    viscous = jnp.pad(coefficients[0], plane_pad)
    velocity = jnp.pad(coefficients[1], plane_pad)
    current = adjoint
    for repeat in range(SWEEPS):
        padded = jnp.pad(current, ((0, 0), (1, 1), (1, 1), (0, 0)))
        current = relax_cells(padded, viscous, velocity, coefficients[2], coefficients[3], coefficients[4])
    weights = current[0]
    bricks = N_GX * N_GY
    slot_brick = jnp.arange(bricks * SLOTS, dtype=jnp.int32) // SLOTS
    first_x = ((slot_brick // N_GY) * CX + slot_corner[0]).astype(jnp.int32)
    first_y = ((slot_brick % N_GY) * CY + slot_corner[1]).astype(jnp.int32)
    first_z = slot_corner[2].astype(jnp.int32)

    def cut_block(start_x, start_y, start_z):
        return lax.dynamic_slice(weights, (start_x, start_y, start_z), (KX, KY, KZ))

    blocks = jax.vmap(cut_block)(first_x, first_y, first_z)
    occupied = slot_turbine >= 0
    safe_ids = jnp.maximum(slot_turbine, 0)
    rotor_data = rotors[:, safe_ids]
    slopes = disk_slopes(blocks, rotor_data[0], rotor_data[1], rotor_data[2], rotor_data[3])
    slopes = jnp.where(occupied[None, :], slopes, jnp.zeros_like(slopes))
    gradient = jnp.zeros((2, TURBINES), jnp.float32).at[:, safe_ids].add(slopes)
    step_taken = jnp.clip(-step_size * gradient, -0.5, 0.5)
    owners = jnp.arange(MOVED, dtype=jnp.int32) // MOVED_DEV
    turbine = owners * TURB_DEV + moved_rotors
    sub_x = rotors[0, turbine] + step_taken[0, turbine]
    sub_y = rotors[1, turbine] + step_taken[1, turbine]
    kernel = disk_shape(sub_x, sub_y, rotors[2, turbine], rotors[3, turbine])[0]
    values = kernel.reshape(MOVED, KX * KY * KZ).astype(jnp.bfloat16)
    target = new_brick[:, 0]
    position = jnp.arange(MOVED, dtype=jnp.int32)
    earlier = position[:, None] > position[None, :]
    slot_rank = jnp.sum(((target[:, None] == target[None, :]) & earlier).astype(jnp.int32), axis=1).astype(jnp.int32)
    row_index = (target * RECV + slot_rank).astype(jnp.int32)
    incoming = jnp.zeros((bricks * RECV, KX * KY * KZ), jnp.bfloat16).at[row_index].set(values)
    return current, step_taken, incoming
```

```python
import functools

import jax
import jax.numpy as jnp
import numpy as np
from jax import lax
from jax.experimental import pallas as pl
from jax.experimental.pallas import tpu as pltpu
from jax.sharding import PartitionSpec as P

KX = 8
KY = 16
KZ = 16
SWEEPS = 2
RECV = 8
EDGE = 16
CHUNK = 8
LANES = 128


TAU = 0.05
SIGMA_AXIAL = 1.5
SIGMA_RADIAL = 4.0
MESH = pl.DeviceIdType.MESH


def sweep_plane(med, src, dst, prev, x, count):
    ahead = jnp.minimum(x + 1, count - 1)
    inside = jnp.where(x + 1 < count, 1.0, 0.0)
    viscous = med[0, x].astype(jnp.float32)
    velocity = med[1, x].astype(jnp.float32)
    reaction = med[2, x].astype(jnp.float32)
    coupling = med[3, x].astype(jnp.float32)
    source = med[4, x].astype(jnp.float32)
    pull = (med[0, ahead].astype(jnp.float32) + med[1, ahead].astype(jnp.float32)) * inside
    diagonal = 6.0 * viscous + velocity + reaction
    rows, cols = viscous.shape
    row = lax.broadcasted_iota(jnp.int32, (rows, cols), 0)
    col = lax.broadcasted_iota(jnp.int32, (rows, cols), 1)
    sides = []
    for c in range(2):
        flux = viscous * src[c, x]
        total = prev[c] + pull * src[c, ahead]
        prev[c] = flux
        total = total + jnp.where(row == 0, 0.0, pltpu.roll(flux, 1, 0))
        total = total + jnp.where(row == rows - 1, 0.0, pltpu.roll(flux, rows - 1, 0))
        total = total + jnp.where(col == 0, 0.0, pltpu.roll(flux, 1, 1))
        total = total + jnp.where(col == cols - 1, 0.0, pltpu.roll(flux, cols - 1, 1))
        sides.append(total)
    k, e = src[0, x], src[1, x]
    dst[0, x] = k + TAU * (source + sides[0] - diagonal * k - coupling * e)
    dst[1, x] = e + TAU * (sides[1] - (diagonal + reaction) * e - coupling * k)


def relax_kernel(
    sizes, q_hbm, med_hbm, out_hbm, q, med, q1, prev, xs, xr, ys, yr, edge_sem, in_sem, out_sem, ssem, rsem
):
    n_gx, n_gy = sizes
    _, count, width, _ = q.shape
    chunks = count // CHUNK
    gx, gy = lax.axis_index("gx"), lax.axis_index("gy")
    x_lo, x_hi = lax.rem(gx + n_gx - 1, n_gx), lax.rem(gx + 1, n_gx)
    y_lo, y_hi = lax.rem(gy + n_gy - 1, n_gy), lax.rem(gy + 1, n_gy)
    peers = ((x_lo, gy), (x_hi, gy), (gx, y_lo), (gx, y_hi))
    mid = pl.ds(EDGE, width - 2 * EDGE)
    edges = (pl.ds(0, EDGE), pl.ds(width - EDGE, EDGE))

    edge_in = []
    for i, part in enumerate(edges):
        edge_in.append(pltpu.make_async_copy(q_hbm.at[:, :, part], q.at[:, :, part], edge_sem.at[i, 0]))
        edge_in.append(
            pltpu.make_async_copy(med_hbm.at[0, :, part], med.at[0, :, part], edge_sem.at[i, 1])
        )

    def chunk_in(i):
        part = pl.ds(i * CHUNK, CHUNK)
        return (
            pltpu.make_async_copy(q_hbm.at[:, part, mid], q.at[:, part, mid], in_sem.at[i, 0]),
            pltpu.make_async_copy(med_hbm.at[0, part, mid], med.at[0, part, mid], in_sem.at[i, 1]),
            pltpu.make_async_copy(
                med_hbm.at[pl.ds(1, 4), part], med.at[pl.ds(1, 4), part], in_sem.at[i, 2]
            ),
        )

    for copy in edge_in:
        copy.start()
    for i in [0, chunks - 1] + list(range(1, chunks - 1)):
        for copy in chunk_in(i):
            copy.start()

    barrier = pltpu.get_barrier_semaphore()
    for peer in peers:
        pl.semaphore_signal(barrier, inc=1, device_id=peer, device_id_type=MESH)
    pl.semaphore_wait(barrier, 4)

    def exchange(turn, src):
        for c in range(2):
            low, high = med[0, 0].astype(jnp.float32), med[0, count - 1].astype(jnp.float32)
            xs[turn, 0, c] = (low + med[1, 0].astype(jnp.float32)) * src[c, 0]
            xs[turn, 1, c] = high * src[c, count - 1]

        copies = []
        for side in range(2):
            copies.append(
                pltpu.make_async_remote_copy(
                    src_ref=xs.at[turn, side],
                    dst_ref=xr.at[turn, side],
                    send_sem=ssem.at[turn, side],
                    recv_sem=rsem.at[turn, side],
                    device_id=peers[side],
                    device_id_type=MESH,
                )
            )
            copies[-1].start()

        @pl.loop(0, count, unroll=4)
        def _(x):
            low = med[0, x, pl.ds(0, EDGE)].astype(jnp.float32)[:8]
            high = med[0, x, pl.ds(width - EDGE, EDGE)].astype(jnp.float32)[8:]
            for c in range(2):
                ys[turn, 0, c, pl.ds(x, 1)] = (low * src[c, x, pl.ds(0, 8)])[:1]
                ys[turn, 1, c, pl.ds(x, 1)] = (high * src[c, x, pl.ds(width - 8, 8)])[7:]

        for side in range(2):
            copies.append(
                pltpu.make_async_remote_copy(
                    src_ref=ys.at[turn, side],
                    dst_ref=yr.at[turn, side],
                    send_sem=ssem.at[turn, 2 + side],
                    recv_sem=rsem.at[turn, 2 + side],
                    device_id=peers[2 + side],
                    device_id_type=MESH,
                )
            )
            copies[-1].start()
        return copies

    def patch(turn, dst):
        has_hi_x = jnp.where(gx < n_gx - 1, TAU, 0.0)
        has_lo_x = jnp.where(gx > 0, TAU, 0.0)
        has_hi_y = jnp.where(gy < n_gy - 1, TAU, 0.0)
        has_lo_y = jnp.where(gy > 0, TAU, 0.0)
        for c in range(2):
            dst[c, count - 1] = dst[c, count - 1] + has_hi_x * xr[turn, 0, c]
            dst[c, 0] = dst[c, 0] + has_lo_x * xr[turn, 1, c]

        @pl.loop(0, count, unroll=4)
        def _(x):
            for c in range(2):
                last = pl.ds(width - 1, 1)
                first = pl.ds(0, 1)
                dst[c, x, last] = dst[c, x, last] + has_hi_y * yr[turn, 0, c, pl.ds(x, 1)]
                dst[c, x, first] = dst[c, x, first] + has_lo_y * yr[turn, 1, c, pl.ds(x, 1)]

    for copy in edge_in:
        copy.wait()
    for i in (0, chunks - 1):
        for copy in chunk_in(i):
            copy.wait()

    copies = exchange(0, q)
    prev[...] = jnp.zeros_like(prev)
    for i in range(chunks):
        if 0 < i + 1 < chunks - 1:
            for copy in chunk_in(i + 1):
                copy.wait()

        @pl.loop(0, CHUNK)
        def _(j):
            sweep_plane(med, q, q1, prev, i * CHUNK + j, count)

    for copy in copies:
        copy.wait()
    patch(0, q1)

    copies = exchange(1, q1)
    prev[...] = jnp.zeros_like(prev)

    def chunk_out(i):
        part = pl.ds(i * CHUNK, CHUNK)
        return pltpu.make_async_copy(q.at[:, part, mid], out_hbm.at[:, part, mid], out_sem.at[i])

    outs = []
    for i in range(chunks):

        @pl.loop(0, CHUNK)
        def _(j):
            sweep_plane(med, q1, q, prev, i * CHUNK + j, count)

        if 0 < i < chunks - 1:
            outs.append(chunk_out(i))
            outs[-1].start()

    for copy in copies:
        copy.wait()
    patch(1, q)
    tail = [chunk_out(0), chunk_out(chunks - 1)]
    for i, part in enumerate(edges):
        sem = out_sem.at[chunks + i]
        tail.append(pltpu.make_async_copy(q.at[:, :, part], out_hbm.at[:, :, part], sem))
    for copy in tail:
        copy.start()
    for copy in outs + tail:
        copy.wait()


def relax(adjoint, medium, sizes):
    channels, count, width, depth = adjoint.shape
    return pl.pallas_call(
        functools.partial(relax_kernel, sizes),
        out_shape=jax.ShapeDtypeStruct(adjoint.shape, jnp.float32),
        in_specs=[pl.BlockSpec(memory_space=pl.ANY)] * 2,
        out_specs=pl.BlockSpec(memory_space=pl.ANY),
        scratch_shapes=[
            pltpu.VMEM(adjoint.shape, jnp.float32),
            pltpu.VMEM(medium.shape, jnp.bfloat16),
            pltpu.VMEM(adjoint.shape, jnp.float32),
            pltpu.VMEM((channels, width, depth), jnp.float32),
            pltpu.VMEM((2, 2, channels, width, depth), jnp.float32),
            pltpu.VMEM((2, 2, channels, width, depth), jnp.float32),
            pltpu.VMEM((2, 2, channels, count, depth), jnp.float32),
            pltpu.VMEM((2, 2, channels, count, depth), jnp.float32),
            pltpu.SemaphoreType.DMA((2, 2)),
            pltpu.SemaphoreType.DMA((count // CHUNK, 3)),
            pltpu.SemaphoreType.DMA((2 + count // CHUNK,)),
            pltpu.SemaphoreType.DMA((2, 4)),
            pltpu.SemaphoreType.DMA((2, 4)),
        ],
        compiler_params=pltpu.CompilerParams(
            collective_id=0, has_side_effects=True, vmem_limit_bytes=48 * 1024 * 1024
        ),
        name="relax",
    )(adjoint, medium)


def z_weights(depth):
    z = np.arange(depth)[:, None] - np.arange(depth)[None, :]
    height = z + 0.5 - KZ / 2.0
    values = np.exp(-(height**2) / (2.0 * SIGMA_RADIAL**2)) * ((z >= 0) & (z < KZ))
    values = values.astype(np.float32)
    high = values.astype(jnp.bfloat16)
    low = (values - high.astype(np.float32)).astype(jnp.bfloat16)
    return np.block([[high, low], [high, np.zeros_like(low)]])


def slope_kernel(
    turb_dev, slot_turbine, corner, table, q_hbm, profile, out_hbm, slopes, q, conv, in_sem, out_sem
):
    _, count, width, depth = q.shape
    chunks = count // CHUNK
    slots = slot_turbine.shape[0]

    def chunk_in(i):
        part = pl.ds(i * CHUNK, CHUNK)
        return pltpu.make_async_copy(q_hbm.at[:, part], q.at[:, part], in_sem.at[i])

    def chunk_out(i):
        part = pl.ds(i * CHUNK, CHUNK)
        return pltpu.make_async_copy(q.at[:, part], out_hbm.at[:, part], out_sem.at[i])

    for i in range(chunks):
        chunk_in(i).start()
    for i in range(chunks):
        chunk_in(i).wait()
        chunk_out(i).start()
        rows = q[0, pl.ds(i * CHUNK, CHUNK)].reshape(CHUNK * width, depth)
        high = rows.astype(jnp.bfloat16)
        low = (rows - high.astype(jnp.float32)).astype(jnp.bfloat16)
        both = jnp.dot(
            jnp.concatenate([high, low], axis=1),
            profile[...],
            preferred_element_type=jnp.float32,
        )
        conv[pl.ds(i * CHUNK, CHUNK)] = (both[:, :depth] + both[:, depth:]).reshape(
            CHUNK, width, depth
        )

    lane = lax.broadcasted_iota(jnp.int32, (1, LANES), 1)
    wide = lax.broadcasted_iota(jnp.int32, (KX * KY, LANES), 1)
    cell = lax.broadcasted_iota(jnp.int32, (KX * KY, LANES), 0)
    cell_x = (cell // KY).astype(jnp.float32) + 0.5 - KX / 2.0
    cell_y = lax.rem(cell, KY).astype(jnp.float32) + 0.5 - KY / 2.0
    for group in range(-(-slots // LANES)):
        start = group * LANES
        stop = min(slots, start + LANES)

        def gather(s, carry):
            values, params = carry
            turbine = jnp.maximum(slot_turbine[s], 0)
            first_x = jnp.minimum(corner[0, s], count - KX)
            first_y = jnp.minimum(corner[1, s], width - KY)
            first_z = jnp.minimum(corner[2, s], depth - KZ)
            block = conv[pl.ds(first_x, KX), pl.ds(first_y, KY)].reshape(KX * KY, depth)
            block = pltpu.roll(block, lax.rem(s - start - first_z + depth, depth), 1)
            mine = lane == s - start
            values = jnp.where(wide == s - start, block, values)
            base = lax.div(turbine, turb_dev) * (5 * turb_dev) + lax.rem(turbine, turb_dev)
            params = tuple(
                jnp.where(mine, table[base + i * turb_dev], p) for i, p in enumerate(params)
            )
            return values, params

        zero = jnp.zeros((1, LANES), jnp.float32)
        values, (sub_x, sub_y, cosine, sine, thrust) = lax.fori_loop(
            start, stop, gather, (jnp.zeros((KX * KY, LANES), jnp.float32), (zero,) * 5), unroll=2
        )
        delta_x, delta_y = cell_x - sub_x, cell_y - sub_y
        along = cosine * delta_x + sine * delta_y
        across = cosine * delta_y - sine * delta_x
        kernel = thrust * jnp.exp(
            -along * along / (2.0 * SIGMA_AXIAL * SIGMA_AXIAL)
            - across * across / (2.0 * SIGMA_RADIAL * SIGMA_RADIAL)
        )
        weighted = kernel * values
        axial = along * (1.0 / (SIGMA_AXIAL * SIGMA_AXIAL))
        radial = across * (1.0 / (SIGMA_RADIAL * SIGMA_RADIAL))
        part = pl.ds(start, LANES)
        slopes[0:1, part] = jnp.sum(
            weighted * (axial * cosine - radial * sine), axis=0, keepdims=True
        )
        slopes[1:2, part] = jnp.sum(
            weighted * (axial * sine + radial * cosine), axis=0, keepdims=True
        )
    for i in range(chunks):
        chunk_out(i).wait()


def slot_slopes(state, slot_turbine, slot_corner, table, turb_dev):
    _, count, width, depth = state.shape
    padded = -(-slot_turbine.shape[0] // LANES) * LANES
    smem = pl.BlockSpec(memory_space=pltpu.SMEM)
    return pl.pallas_call(
        functools.partial(slope_kernel, turb_dev),
        out_shape=(
            jax.ShapeDtypeStruct(state.shape, jnp.float32),
            jax.ShapeDtypeStruct((2, padded), jnp.float32),
        ),
        in_specs=[
            smem,
            smem,
            smem,
            pl.BlockSpec(memory_space=pl.ANY),
            pl.BlockSpec(memory_space=pltpu.VMEM),
        ],
        out_specs=(
            pl.BlockSpec(memory_space=pl.ANY),
            pl.BlockSpec(memory_space=pltpu.VMEM),
        ),
        scratch_shapes=[
            pltpu.VMEM(state.shape, jnp.float32),
            pltpu.VMEM((count, width, depth), jnp.float32),
            pltpu.SemaphoreType.DMA((count // CHUNK,)),
            pltpu.SemaphoreType.DMA((count // CHUNK,)),
        ],
        compiler_params=pltpu.CompilerParams(vmem_limit_bytes=40 * 1024 * 1024),
        name="slopes",
    )(slot_turbine, slot_corner, table, state, jnp.asarray(z_weights(depth)))


def finish_kernel(
    sizes, turb_dev, step_size, slopes, ids, moved, step_out, incoming, every, ssem, rsem
):
    n_gx, n_gy = sizes
    n = n_gx * n_gy
    gx, gy = lax.axis_index("gx"), lax.axis_index("gy")
    me = gx * n_gy + gy
    padded = slopes.shape[1]
    barrier = pltpu.get_barrier_semaphore()

    def peer(i):
        other = lax.rem(me + i, n)
        return (lax.div(other, n_gy), lax.rem(other, n_gy))

    @pl.loop(1, n)
    def _(i):
        pl.semaphore_signal(barrier, inc=1, device_id=peer(i), device_id_type=MESH)

    pl.semaphore_wait(barrier, n - 1)

    def send(i):
        return pltpu.make_async_remote_copy(
            src_ref=slopes,
            dst_ref=every.at[me],
            send_sem=ssem.at[i],
            recv_sem=rsem.at[me],
            device_id=peer(i),
            device_id_type=MESH,
        )

    @pl.loop(1, n)
    def _(i):
        send(i).start()

    every[me] = slopes[...]

    total = moved.shape[1]
    mine = (moved[0:1] == me.astype(jnp.float32)).astype(jnp.float32)
    before = lax.broadcasted_iota(jnp.int32, (total, total), 0) < lax.broadcasted_iota(
        jnp.int32, (total, total), 1
    )
    rank = jnp.dot(
        jnp.broadcast_to(mine, (RECV, total)).astype(jnp.bfloat16),
        before.astype(jnp.float32).astype(jnp.bfloat16),
        preferred_element_type=jnp.float32,
    )
    slot = lax.broadcasted_iota(jnp.int32, (RECV, total), 0).astype(jnp.float32)
    chosen = jnp.where((rank == slot) & (jnp.broadcast_to(mine, (RECV, total)) > 0), 1.0, 0.0)
    valid = jnp.sum(chosen, axis=1, keepdims=True)
    fields = [jnp.sum(chosen * moved[i : i + 1], axis=1, keepdims=True) for i in range(1, 7)]
    wanted, sub_x, sub_y, cosine, sine, thrust = fields
    own = (
        me * turb_dev + lax.broadcasted_iota(jnp.int32, (turb_dev, padded), 0)
    ).astype(jnp.float32)
    targets = jnp.concatenate([own, jnp.broadcast_to(wanted, (RECV, padded))], axis=0)

    @pl.loop(1, n)
    def _(i):
        send(i).wait_send()
        other = lax.rem(me + i, n)
        pltpu.make_async_remote_copy(
            src_ref=slopes,
            dst_ref=every.at[other],
            send_sem=ssem.at[i],
            recv_sem=rsem.at[other],
            device_id=peer(i),
            device_id_type=MESH,
        ).wait_recv()

    def collect(d, carry):
        sum_x, sum_y = carry
        hit = targets == ids[d]
        both = every[d]
        return (
            sum_x + jnp.where(hit, both[0:1], 0.0),
            sum_y + jnp.where(hit, both[1:2], 0.0),
        )

    zero = jnp.zeros((turb_dev + RECV, padded), jnp.float32)
    sums = lax.fori_loop(0, n, collect, (zero, zero), unroll=2)
    step = step_size[0]
    taken = [
        jnp.clip(-step * jnp.sum(part, axis=1, keepdims=True), -0.5, 0.5) for part in sums
    ]
    flip = lax.broadcasted_iota(jnp.int32, (turb_dev, turb_dev), 0) == lax.broadcasted_iota(
        jnp.int32, (turb_dev, turb_dev), 1
    )
    for i in range(2):
        step_out[i : i + 1] = jnp.sum(
            jnp.where(flip, taken[i][:turb_dev], 0.0), axis=0, keepdims=True
        )
    cells = KX * KY * KZ
    cell = lax.broadcasted_iota(jnp.int32, (RECV, cells), 1)
    ex = (cell // (KY * KZ)).astype(jnp.float32) + 0.5 - KX / 2.0
    ey = lax.rem(cell // KZ, KY).astype(jnp.float32) + 0.5 - KY / 2.0
    ez = lax.rem(cell, KZ).astype(jnp.float32) + 0.5 - KZ / 2.0
    delta_x = ex - (sub_x + taken[0][turb_dev:])
    delta_y = ey - (sub_y + taken[1][turb_dev:])
    along = cosine * delta_x + sine * delta_y
    across = cosine * delta_y - sine * delta_x
    kernel = thrust * jnp.exp(
        -along * along / (2.0 * SIGMA_AXIAL * SIGMA_AXIAL)
        - (across * across + ez * ez) / (2.0 * SIGMA_RADIAL * SIGMA_RADIAL)
    )
    incoming[...] = jnp.where(valid > 0, kernel, 0.0).astype(jnp.bfloat16)


def finish(step_size, slopes, ids, moved, turb_dev, sizes):
    n = sizes[0] * sizes[1]
    vmem = pl.BlockSpec(memory_space=pltpu.VMEM)

    def kernel(step_ref, slopes_ref, ids_ref, moved_ref, *rest):
        finish_kernel(sizes, turb_dev, step_ref, slopes_ref, ids_ref, moved_ref, *rest)

    return pl.pallas_call(
        kernel,
        out_shape=(
            jax.ShapeDtypeStruct((2, turb_dev), jnp.float32),
            jax.ShapeDtypeStruct((RECV, KX * KY * KZ), jnp.bfloat16),
        ),
        in_specs=[pl.BlockSpec(memory_space=pltpu.SMEM), vmem, vmem, vmem],
        out_specs=(vmem, vmem),
        scratch_shapes=[
            pltpu.VMEM((n,) + slopes.shape, jnp.float32),
            pltpu.SemaphoreType.DMA((n,)),
            pltpu.SemaphoreType.DMA((n,)),
        ],
        compiler_params=pltpu.CompilerParams(collective_id=1, has_side_effects=True),
        name="finish",
    )(step_size, slopes, ids, moved)


def body(
    sizes, adjoint, medium, rotors, step_size, slot_turbine, slot_corner, moved_rotors, new_brick
):
    turb_dev = rotors.shape[1]
    slots = slot_turbine.shape[0]
    padded = -(-slots // LANES) * LANES
    moved_dev = moved_rotors.shape[0]
    brick = lax.axis_index("gx") * sizes[1] + lax.axis_index("gy")
    full = jnp.stack([rotors[0], rotors[1], jnp.cos(rotors[2]), jnp.sin(rotors[2]), rotors[3]])
    picked = (moved_rotors[:, None] == jnp.arange(turb_dev)[None, :])[None]
    picked = jnp.sum(jnp.where(picked, full[:, None, :], 0.0), axis=2)
    fields = jnp.concatenate(
        [
            new_brick[:, 0].astype(jnp.float32)[None],
            (brick * turb_dev + moved_rotors).astype(jnp.float32)[None],
            picked,
        ]
    )
    ids = jnp.pad(slot_turbine.astype(jnp.float32), (0, padded - slots), constant_values=-1.0)
    packed = jnp.concatenate([full.reshape(-1), ids, fields.reshape(-1)])
    packed = jnp.pad(packed, (0, -packed.shape[0] % LANES))
    every = lax.all_gather(packed, ("gx", "gy"), axis=0)
    n = every.shape[0]
    cut = 5 * turb_dev
    table = every[:, :cut].reshape(-1)
    every_ids = every[:, None, cut : cut + padded]
    every_moved = every[:, cut + padded : cut + padded + 7 * moved_dev]
    every_moved = every_moved.reshape(n, 7, moved_dev).transpose(1, 0, 2).reshape(7, n * moved_dev)

    state = relax(adjoint, medium, sizes)
    state, slopes = slot_slopes(state, slot_turbine, slot_corner, table, turb_dev)
    step_taken, incoming = finish(
        step_size.reshape(1), slopes, every_ids, every_moved, turb_dev, sizes
    )
    return (state, step_taken, incoming)


def solution(mesh):
    sizes = (mesh.shape["gx"], mesh.shape["gy"])
    return jax.shard_map(
        functools.partial(body, sizes),
        mesh=mesh,
        in_specs=(
            P(None, "gx", "gy", None),
            P(None, "gx", "gy", None),
            P(None, ("gx", "gy")),
            P(),
            P(("gx", "gy")),
            P(None, ("gx", "gy")),
            P(("gx", "gy")),
            P(("gx", "gy"), None),
        ),
        out_specs=(P(None, "gx", "gy", None), P(None, ("gx", "gy")), P(("gx", "gy"), None)),
        check_vma=False,
    )
```

```python
import functools

import jax
import jax.numpy as jnp
import numpy as np
from jax import lax
from jax.experimental import pallas as pl
from jax.experimental.pallas import tpu as pltpu
from jax.sharding import PartitionSpec as P

KX = 8
KY = 16
KZ = 16
SWEEPS = 2
RECV = 8
EDGE = 16
CHUNK = 8
LANES = 128


TAU = 0.05
SIGMA_AXIAL = 1.5
SIGMA_RADIAL = 4.0
MESH = pl.DeviceIdType.MESH


def sweep_plane(med, src, dst, prev, x, count):
    ahead = jnp.minimum(x + 1, count - 1)
    inside = jnp.where(x + 1 < count, 1.0, 0.0)
    viscous = med[0, x].astype(jnp.float32)
    velocity = med[1, x].astype(jnp.float32)
    reaction = med[2, x].astype(jnp.float32)
    coupling = med[3, x].astype(jnp.float32)
    source = med[4, x].astype(jnp.float32)
    pull = (med[0, ahead].astype(jnp.float32) + med[1, ahead].astype(jnp.float32)) * inside
    diagonal = 6.0 * viscous + velocity + reaction
    rows, cols = viscous.shape
    row = lax.broadcasted_iota(jnp.int32, (rows, cols), 0)
    col = lax.broadcasted_iota(jnp.int32, (rows, cols), 1)
    sides = []
    for c in range(2):
        flux = viscous * src[c, x]
        total = prev[c] + pull * src[c, ahead]
        prev[c] = flux
        total = total + jnp.where(row == 0, 0.0, pltpu.roll(flux, 1, 0))
        total = total + jnp.where(row == rows - 1, 0.0, pltpu.roll(flux, rows - 1, 0))
        total = total + jnp.where(col == 0, 0.0, pltpu.roll(flux, 1, 1))
        total = total + jnp.where(col == cols - 1, 0.0, pltpu.roll(flux, cols - 1, 1))
        sides.append(total)
    k, e = src[0, x], src[1, x]
    dst[0, x] = k + TAU * (source + sides[0] - diagonal * k - coupling * e)
    dst[1, x] = e + TAU * (sides[1] - (diagonal + reaction) * e - coupling * k)


def pack_tables(me, rotors, listed, moved, target, pack):
    turb_dev, slots, moved_dev = rotors.shape[1], listed.shape[1], moved.shape[0]
    pack[...] = jnp.full(pack.shape, -1.0, jnp.float32)
    own = pl.ds(0, turb_dev)
    pack[0:2, own] = rotors[0:2]
    pack[2:3, own] = jnp.cos(rotors[2:3])
    pack[3:4, own] = jnp.sin(rotors[2:3])
    pack[4:5, own] = rotors[3:4]
    for group in range(-(-slots // LANES)):
        size = min(LANES, slots - group * LANES)
        pack[5 + group : 6 + group, pl.ds(0, size)] = listed[
            :, pl.ds(group * LANES, size)
        ].astype(jnp.float32)
    full = pack[...]
    lane = lax.broadcasted_iota(jnp.int32, full.shape, 1)
    field = lax.broadcasted_iota(jnp.int32, full.shape, 0) + 2
    line = jnp.full((1, LANES), -1.0, jnp.float32)
    for j in range(moved_dev):
        picked = jnp.sum(jnp.where(lane == moved[j], full, 0.0), axis=1, keepdims=True)
        here = (lane == moved_dev * field + j) & (field < 7)
        spread = jnp.sum(jnp.where(here, picked, 0.0), axis=0, keepdims=True)
        place = lane[0:1]
        for f in range(2, 7):
            line = jnp.where(place == moved_dev * f + j, spread, line)
        line = jnp.where(place == j, target[j, 0].astype(jnp.float32), line)
        number = (me * turb_dev + moved[j]).astype(jnp.float32)
        line = jnp.where(place == moved_dev + j, number, line)
    pack[7:8] = line


def relax_kernel(
    sizes,
    rotors,
    listed,
    moved,
    target,
    q_hbm,
    med_hbm,
    out_hbm,
    every,
    q,
    med,
    q1,
    prev,
    xs,
    xr,
    ys,
    yr,
    pack,
    table,
    edge_sem,
    in_sem,
    out_sem,
    ssem,
    rsem,
    tsend,
    trecv,
):
    n_gx, n_gy = sizes
    n = n_gx * n_gy
    _, count, width, _ = q.shape
    chunks = count // CHUNK
    gx, gy = lax.axis_index("gx"), lax.axis_index("gy")
    x_lo, x_hi = lax.rem(gx + n_gx - 1, n_gx), lax.rem(gx + 1, n_gx)
    y_lo, y_hi = lax.rem(gy + n_gy - 1, n_gy), lax.rem(gy + 1, n_gy)
    peers = ((x_lo, gy), (x_hi, gy), (gx, y_lo), (gx, y_hi))
    mid = pl.ds(EDGE, width - 2 * EDGE)
    edges = (pl.ds(0, EDGE), pl.ds(width - EDGE, EDGE))

    edge_in = []
    for i, part in enumerate(edges):
        edge_in.append(pltpu.make_async_copy(q_hbm.at[:, :, part], q.at[:, :, part], edge_sem.at[i, 0]))
        edge_in.append(
            pltpu.make_async_copy(med_hbm.at[0, :, part], med.at[0, :, part], edge_sem.at[i, 1])
        )

    def chunk_in(i):
        part = pl.ds(i * CHUNK, CHUNK)
        return (
            pltpu.make_async_copy(q_hbm.at[:, part, mid], q.at[:, part, mid], in_sem.at[i, 0]),
            pltpu.make_async_copy(med_hbm.at[0, part, mid], med.at[0, part, mid], in_sem.at[i, 1]),
            pltpu.make_async_copy(
                med_hbm.at[pl.ds(1, 4), part], med.at[pl.ds(1, 4), part], in_sem.at[i, 2]
            ),
        )

    for copy in edge_in:
        copy.start()
    for i in [0, chunks - 1] + list(range(1, chunks - 1)):
        for copy in chunk_in(i):
            copy.start()

    barrier = pltpu.get_barrier_semaphore()
    me = gx * n_gy + gy

    @pl.loop(1, n)
    def _(i):
        other = lax.rem(me + i, n)
        pl.semaphore_signal(
            barrier,
            inc=1,
            device_id=(lax.div(other, n_gy), lax.rem(other, n_gy)),
            device_id_type=MESH,
        )

    pack_tables(me, rotors, listed, moved, target, pack)
    pl.semaphore_wait(barrier, n - 1)

    def share(i, place):
        other = lax.rem(me + i, n)
        return pltpu.make_async_remote_copy(
            src_ref=pack,
            dst_ref=table.at[place],
            send_sem=tsend.at[i],
            recv_sem=trecv.at[place],
            device_id=(lax.div(other, n_gy), lax.rem(other, n_gy)),
            device_id_type=MESH,
        )

    def exchange(turn, src):
        for c in range(2):
            low, high = med[0, 0].astype(jnp.float32), med[0, count - 1].astype(jnp.float32)
            xs[turn, 0, c] = (low + med[1, 0].astype(jnp.float32)) * src[c, 0]
            xs[turn, 1, c] = high * src[c, count - 1]

        copies = []
        for side in range(2):
            copies.append(
                pltpu.make_async_remote_copy(
                    src_ref=xs.at[turn, side],
                    dst_ref=xr.at[turn, side],
                    send_sem=ssem.at[turn, side],
                    recv_sem=rsem.at[turn, side],
                    device_id=peers[side],
                    device_id_type=MESH,
                )
            )
            copies[-1].start()

        @pl.loop(0, count, unroll=4)
        def _(x):
            low = med[0, x, pl.ds(0, EDGE)].astype(jnp.float32)[:8]
            high = med[0, x, pl.ds(width - EDGE, EDGE)].astype(jnp.float32)[8:]
            for c in range(2):
                ys[turn, 0, c, pl.ds(x, 1)] = (low * src[c, x, pl.ds(0, 8)])[:1]
                ys[turn, 1, c, pl.ds(x, 1)] = (high * src[c, x, pl.ds(width - 8, 8)])[7:]

        for side in range(2):
            copies.append(
                pltpu.make_async_remote_copy(
                    src_ref=ys.at[turn, side],
                    dst_ref=yr.at[turn, side],
                    send_sem=ssem.at[turn, 2 + side],
                    recv_sem=rsem.at[turn, 2 + side],
                    device_id=peers[2 + side],
                    device_id_type=MESH,
                )
            )
            copies[-1].start()
        return copies

    def patch(turn, dst):
        has_hi_x = jnp.where(gx < n_gx - 1, TAU, 0.0)
        has_lo_x = jnp.where(gx > 0, TAU, 0.0)
        has_hi_y = jnp.where(gy < n_gy - 1, TAU, 0.0)
        has_lo_y = jnp.where(gy > 0, TAU, 0.0)
        for c in range(2):
            dst[c, count - 1] = dst[c, count - 1] + has_hi_x * xr[turn, 0, c]
            dst[c, 0] = dst[c, 0] + has_lo_x * xr[turn, 1, c]

        @pl.loop(0, count, unroll=4)
        def _(x):
            for c in range(2):
                last = pl.ds(width - 1, 1)
                first = pl.ds(0, 1)
                dst[c, x, last] = dst[c, x, last] + has_hi_y * yr[turn, 0, c, pl.ds(x, 1)]
                dst[c, x, first] = dst[c, x, first] + has_lo_y * yr[turn, 1, c, pl.ds(x, 1)]

    for copy in edge_in:
        copy.wait()
    for i in (0, chunks - 1):
        for copy in chunk_in(i):
            copy.wait()

    copies = exchange(0, q)

    @pl.loop(1, n)
    def _(i):
        share(i, me).start()

    table[me] = pack[...]
    prev[...] = jnp.zeros_like(prev)
    for i in range(chunks):
        if 0 < i + 1 < chunks - 1:
            for copy in chunk_in(i + 1):
                copy.wait()

        @pl.loop(0, CHUNK)
        def _(j):
            sweep_plane(med, q, q1, prev, i * CHUNK + j, count)

    for copy in copies:
        copy.wait()
    patch(0, q1)

    copies = exchange(1, q1)
    prev[...] = jnp.zeros_like(prev)

    def chunk_out(i):
        part = pl.ds(i * CHUNK, CHUNK)
        return pltpu.make_async_copy(q.at[:, part, mid], out_hbm.at[:, part, mid], out_sem.at[i])

    outs = []
    for i in range(chunks):

        @pl.loop(0, CHUNK)
        def _(j):
            sweep_plane(med, q1, q, prev, i * CHUNK + j, count)

        if 0 < i < chunks - 1:
            outs.append(chunk_out(i))
            outs[-1].start()

    @pl.loop(1, n)
    def _(i):
        share(i, me).wait_send()
        share(i, lax.rem(me + i, n)).wait_recv()

    every[...] = table[...]
    for copy in copies:
        copy.wait()
    patch(1, q)
    tail = [chunk_out(0), chunk_out(chunks - 1)]
    for i, part in enumerate(edges):
        sem = out_sem.at[chunks + i]
        tail.append(pltpu.make_async_copy(q.at[:, :, part], out_hbm.at[:, :, part], sem))
    for copy in tail:
        copy.start()
    for copy in outs + tail:
        copy.wait()


def relax(adjoint, medium, rotors, slot_turbine, moved_rotors, new_brick, sizes):
    n = sizes[0] * sizes[1]
    vmem, smem = pl.BlockSpec(memory_space=pltpu.VMEM), pl.BlockSpec(memory_space=pltpu.SMEM)
    channels, count, width, depth = adjoint.shape
    return pl.pallas_call(
        functools.partial(relax_kernel, sizes),
        out_shape=(
            jax.ShapeDtypeStruct(adjoint.shape, jnp.float32),
            jax.ShapeDtypeStruct((n, 8, LANES), jnp.float32),
        ),
        in_specs=[vmem, vmem, smem, smem] + [pl.BlockSpec(memory_space=pl.ANY)] * 2,
        out_specs=(pl.BlockSpec(memory_space=pl.ANY), vmem),
        scratch_shapes=[
            pltpu.VMEM(adjoint.shape, jnp.float32),
            pltpu.VMEM(medium.shape, jnp.bfloat16),
            pltpu.VMEM(adjoint.shape, jnp.float32),
            pltpu.VMEM((channels, width, depth), jnp.float32),
            pltpu.VMEM((2, 2, channels, width, depth), jnp.float32),
            pltpu.VMEM((2, 2, channels, width, depth), jnp.float32),
            pltpu.VMEM((2, 2, channels, count, depth), jnp.float32),
            pltpu.VMEM((2, 2, channels, count, depth), jnp.float32),
            pltpu.VMEM((8, LANES), jnp.float32),
            pltpu.VMEM((n, 8, LANES), jnp.float32),
            pltpu.SemaphoreType.DMA((2, 2)),
            pltpu.SemaphoreType.DMA((count // CHUNK, 3)),
            pltpu.SemaphoreType.DMA((2 + count // CHUNK,)),
            pltpu.SemaphoreType.DMA((2, 4)),
            pltpu.SemaphoreType.DMA((2, 4)),
            pltpu.SemaphoreType.DMA((n,)),
            pltpu.SemaphoreType.DMA((n,)),
        ],
        compiler_params=pltpu.CompilerParams(
            collective_id=0, has_side_effects=True, vmem_limit_bytes=48 * 1024 * 1024
        ),
        name="relax",
    )(rotors, slot_turbine[None, :], moved_rotors, new_brick, adjoint, medium)


def z_weights(depth):
    z = np.arange(depth)[:, None] - np.arange(depth)[None, :]
    height = z + 0.5 - KZ / 2.0
    values = np.exp(-(height**2) / (2.0 * SIGMA_RADIAL**2)) * ((z >= 0) & (z < KZ))
    values = values.astype(np.float32)
    high = values.astype(jnp.bfloat16)
    low = (values - high.astype(np.float32)).astype(jnp.bfloat16)
    return np.block([[high, low], [high, np.zeros_like(low)]])


def slope_kernel(
    turb_dev,
    slot_turbine,
    corner,
    table_hbm,
    q_hbm,
    profile,
    out_hbm,
    slopes,
    q,
    conv,
    table,
    table_sem,
    in_sem,
    out_sem,
):
    _, count, width, depth = q.shape
    chunks = count // CHUNK
    slots = slot_turbine.shape[0]

    def chunk_in(i):
        part = pl.ds(i * CHUNK, CHUNK)
        return pltpu.make_async_copy(q_hbm.at[:, part], q.at[:, part], in_sem.at[i])

    def chunk_out(i):
        part = pl.ds(i * CHUNK, CHUNK)
        return pltpu.make_async_copy(q.at[:, part], out_hbm.at[:, part], out_sem.at[i])

    fetch = pltpu.make_async_copy(table_hbm, table, table_sem)
    fetch.start()
    for i in range(chunks):
        chunk_in(i).start()
    for i in range(chunks):
        chunk_in(i).wait()
        chunk_out(i).start()
        rows = q[0, pl.ds(i * CHUNK, CHUNK)].reshape(CHUNK * width, depth)
        high = rows.astype(jnp.bfloat16)
        low = (rows - high.astype(jnp.float32)).astype(jnp.bfloat16)
        both = jnp.dot(
            jnp.concatenate([high, low], axis=1),
            profile[...],
            preferred_element_type=jnp.float32,
        )
        conv[pl.ds(i * CHUNK, CHUNK)] = (both[:, :depth] + both[:, depth:]).reshape(
            CHUNK, width, depth
        )

    fetch.wait()
    slopes[...] = jnp.zeros_like(slopes)
    groups = -(-slots // LANES)
    lane = lax.broadcasted_iota(jnp.int32, (1, LANES), 1)
    wide = lax.broadcasted_iota(jnp.int32, (KX * KY, LANES), 1)
    cell = lax.broadcasted_iota(jnp.int32, (KX * KY, LANES), 0)
    cell_x = (cell // KY).astype(jnp.float32) + 0.5 - KX / 2.0
    cell_y = lax.rem(cell, KY).astype(jnp.float32) + 0.5 - KY / 2.0
    for group in range(groups):
        start = group * LANES
        stop = min(slots, start + LANES)

        def gather(s, carry):
            values, params = carry
            turbine = jnp.maximum(slot_turbine[s], 0)
            first_x = jnp.minimum(corner[0, s], count - KX)
            first_y = jnp.minimum(corner[1, s], width - KY)
            first_z = jnp.minimum(corner[2, s], depth - KZ)
            block = conv[pl.ds(first_x, KX), pl.ds(first_y, KY)].reshape(KX * KY, depth)
            block = pltpu.roll(block, lax.rem(s - start - first_z + depth, depth), 1)
            mine = lane == s - start
            values = jnp.where(wide == s - start, block, values)
            owner, local = lax.div(turbine, turb_dev), lax.rem(turbine, turb_dev)
            params = tuple(
                jnp.where(mine, table[owner, i, local], p) for i, p in enumerate(params)
            )
            return values, params

        zero = jnp.zeros((1, LANES), jnp.float32)
        values, (sub_x, sub_y, cosine, sine, thrust) = lax.fori_loop(
            start, stop, gather, (jnp.zeros((KX * KY, LANES), jnp.float32), (zero,) * 5), unroll=2
        )
        delta_x, delta_y = cell_x - sub_x, cell_y - sub_y
        along = cosine * delta_x + sine * delta_y
        across = cosine * delta_y - sine * delta_x
        kernel = thrust * jnp.exp(
            -along * along / (2.0 * SIGMA_AXIAL * SIGMA_AXIAL)
            - across * across / (2.0 * SIGMA_RADIAL * SIGMA_RADIAL)
        )
        weighted = kernel * values
        axial = along * (1.0 / (SIGMA_AXIAL * SIGMA_AXIAL))
        radial = across * (1.0 / (SIGMA_RADIAL * SIGMA_RADIAL))
        other = groups + group
        slopes[group : group + 1] = jnp.sum(
            weighted * (axial * cosine - radial * sine), axis=0, keepdims=True
        )
        slopes[other : other + 1] = jnp.sum(
            weighted * (axial * sine + radial * cosine), axis=0, keepdims=True
        )
    for i in range(chunks):
        chunk_out(i).wait()


def slot_slopes(state, slot_turbine, slot_corner, table, turb_dev):
    _, count, width, depth = state.shape
    smem = pl.BlockSpec(memory_space=pltpu.SMEM)
    return pl.pallas_call(
        functools.partial(slope_kernel, turb_dev),
        out_shape=(
            jax.ShapeDtypeStruct(state.shape, jnp.float32),
            jax.ShapeDtypeStruct((8, LANES), jnp.float32),
        ),
        in_specs=[
            smem,
            smem,
            pl.BlockSpec(memory_space=pl.ANY),
            pl.BlockSpec(memory_space=pl.ANY),
            pl.BlockSpec(memory_space=pltpu.VMEM),
        ],
        out_specs=(
            pl.BlockSpec(memory_space=pl.ANY),
            pl.BlockSpec(memory_space=pltpu.VMEM),
        ),
        scratch_shapes=[
            pltpu.VMEM(state.shape, jnp.float32),
            pltpu.VMEM((count, width, depth), jnp.float32),
            pltpu.SMEM(table.shape, jnp.float32),
            pltpu.SemaphoreType.DMA,
            pltpu.SemaphoreType.DMA((count // CHUNK,)),
            pltpu.SemaphoreType.DMA((count // CHUNK,)),
        ],
        compiler_params=pltpu.CompilerParams(vmem_limit_bytes=58 * 1024 * 1024),
        name="slopes",
    )(slot_turbine, slot_corner, table, state, jnp.asarray(z_weights(depth)))


def finish_kernel(
    sizes, groups, moved_dev, step_size, slopes, table, step_out, incoming, every, ssem, rsem
):
    n_gx, n_gy = sizes
    n = n_gx * n_gy
    gx, gy = lax.axis_index("gx"), lax.axis_index("gy")
    me = gx * n_gy + gy
    turb_dev = step_out.shape[1]
    barrier = pltpu.get_barrier_semaphore()

    def peer(i):
        other = lax.rem(me + i, n)
        return (lax.div(other, n_gy), lax.rem(other, n_gy))

    @pl.loop(1, n)
    def _(i):
        pl.semaphore_signal(barrier, inc=1, device_id=peer(i), device_id_type=MESH)

    pl.semaphore_wait(barrier, n - 1)

    def send(i):
        return pltpu.make_async_remote_copy(
            src_ref=slopes,
            dst_ref=every.at[me],
            send_sem=ssem.at[i],
            recv_sem=rsem.at[me],
            device_id=peer(i),
            device_id_type=MESH,
        )

    @pl.loop(1, n)
    def _(i):
        send(i).start()

    every[me] = slopes[...]

    lines = table[:, 7]
    lane = lax.broadcasted_iota(jnp.int32, lines.shape, 1)
    mine = jnp.where((lines == me.astype(jnp.float32)) & (lane < moved_dev), 1.0, 0.0)

    def earlier(size, row, col):
        less = lax.broadcasted_iota(jnp.int32, (size, size), row) < lax.broadcasted_iota(
            jnp.int32, (size, size), col
        )
        return jnp.where(less, 1.0, 0.0).astype(jnp.bfloat16)

    rank = jnp.sum(
        jnp.dot(
            earlier(n, 1, 0), mine.astype(jnp.bfloat16), preferred_element_type=jnp.float32
        ),
        axis=1,
        keepdims=True,
    ) + jnp.dot(
        mine.astype(jnp.bfloat16), earlier(LANES, 0, 1), preferred_element_type=jnp.float32
    )
    shifted = [pltpu.roll(lines, LANES - moved_dev * f, 1) for f in range(1, 7)]
    chosen = [jnp.where(rank == float(slot), mine, 0.0) for slot in range(RECV)]

    def per_slot(values):
        parts = [jnp.sum(pick * values, axis=0, keepdims=True) for pick in chosen]
        return jnp.sum(jnp.concatenate(parts, axis=0), axis=1, keepdims=True)

    valid = per_slot(jnp.ones_like(lines))
    wanted, sub_x, sub_y, cosine, sine, thrust = [per_slot(values) for values in shifted]
    own = (
        me * turb_dev + lax.broadcasted_iota(jnp.int32, (turb_dev, LANES), 0)
    ).astype(jnp.float32)
    targets = jnp.concatenate([own, jnp.broadcast_to(wanted, (RECV, LANES))], axis=0)

    @pl.loop(1, n)
    def _(i):
        send(i).wait_send()
        other = lax.rem(me + i, n)
        pltpu.make_async_remote_copy(
            src_ref=slopes,
            dst_ref=every.at[other],
            send_sem=ssem.at[i],
            recv_sem=rsem.at[other],
            device_id=peer(i),
            device_id_type=MESH,
        ).wait_recv()

    def collect(d, carry):
        sum_x, sum_y = carry
        for group in range(groups):
            hit = targets == table[d, pl.ds(5 + group, 1)]
            sum_x = sum_x + jnp.where(hit, every[d, pl.ds(group, 1)], 0.0)
            sum_y = sum_y + jnp.where(hit, every[d, pl.ds(groups + group, 1)], 0.0)
        return sum_x, sum_y

    zero = jnp.zeros((turb_dev + RECV, LANES), jnp.float32)
    sums = lax.fori_loop(0, n, collect, (zero, zero), unroll=2)
    step = step_size[0]
    taken = [
        jnp.clip(-step * jnp.sum(part, axis=1, keepdims=True), -0.5, 0.5) for part in sums
    ]
    flip = lax.broadcasted_iota(jnp.int32, (turb_dev, turb_dev), 0) == lax.broadcasted_iota(
        jnp.int32, (turb_dev, turb_dev), 1
    )
    for i in range(2):
        step_out[i : i + 1] = jnp.sum(
            jnp.where(flip, taken[i][:turb_dev], 0.0), axis=0, keepdims=True
        )
    cells = KX * KY * KZ
    cell = lax.broadcasted_iota(jnp.int32, (RECV, cells), 1)
    ex = (cell // (KY * KZ)).astype(jnp.float32) + 0.5 - KX / 2.0
    ey = lax.rem(cell // KZ, KY).astype(jnp.float32) + 0.5 - KY / 2.0
    ez = lax.rem(cell, KZ).astype(jnp.float32) + 0.5 - KZ / 2.0
    delta_x = ex - (sub_x + taken[0][turb_dev:])
    delta_y = ey - (sub_y + taken[1][turb_dev:])
    along = cosine * delta_x + sine * delta_y
    across = cosine * delta_y - sine * delta_x
    kernel = thrust * jnp.exp(
        -along * along / (2.0 * SIGMA_AXIAL * SIGMA_AXIAL)
        - (across * across + ez * ez) / (2.0 * SIGMA_RADIAL * SIGMA_RADIAL)
    )
    incoming[...] = jnp.where(valid > 0, kernel, 0.0).astype(jnp.bfloat16)


def finish(step_size, slopes, table, turb_dev, groups, moved_dev, sizes):
    n = sizes[0] * sizes[1]
    vmem = pl.BlockSpec(memory_space=pltpu.VMEM)

    return pl.pallas_call(
        functools.partial(finish_kernel, sizes, groups, moved_dev),
        out_shape=(
            jax.ShapeDtypeStruct((2, turb_dev), jnp.float32),
            jax.ShapeDtypeStruct((RECV, KX * KY * KZ), jnp.bfloat16),
        ),
        in_specs=[pl.BlockSpec(memory_space=pltpu.SMEM), vmem, vmem],
        out_specs=(vmem, vmem),
        scratch_shapes=[
            pltpu.VMEM((n,) + slopes.shape, jnp.float32),
            pltpu.SemaphoreType.DMA((n,)),
            pltpu.SemaphoreType.DMA((n,)),
        ],
        compiler_params=pltpu.CompilerParams(collective_id=1, has_side_effects=True),
        name="finish",
    )(step_size, slopes, table)


def body(
    sizes, adjoint, medium, rotors, step_size, slot_turbine, slot_corner, moved_rotors, new_brick
):
    turb_dev = rotors.shape[1]
    groups = -(-slot_turbine.shape[0] // LANES)
    state, table = relax(adjoint, medium, rotors, slot_turbine, moved_rotors, new_brick, sizes)
    state, slopes = slot_slopes(state, slot_turbine, slot_corner, table, turb_dev)
    step_taken, incoming = finish(
        step_size.reshape(1), slopes, table, turb_dev, groups, moved_rotors.shape[0], sizes
    )
    return (state, step_taken, incoming)


def solution(mesh):
    sizes = (mesh.shape["gx"], mesh.shape["gy"])
    return jax.shard_map(
        functools.partial(body, sizes),
        mesh=mesh,
        in_specs=(
            P(None, "gx", "gy", None),
            P(None, "gx", "gy", None),
            P(None, ("gx", "gy")),
            P(),
            P(("gx", "gy")),
            P(None, ("gx", "gy")),
            P(("gx", "gy")),
            P(("gx", "gy"), None),
        ),
        out_specs=(P(None, "gx", "gy", None), P(None, ("gx", "gy")), P(("gx", "gy"), None)),
        check_vma=False,
    )
```

```python
import functools

import jax
import jax.numpy as jnp
import numpy as np
from jax import lax
from jax.experimental import pallas as pl
from jax.experimental.pallas import tpu as pltpu
from jax.sharding import PartitionSpec as P

KX = 8
KY = 16
KZ = 16
SWEEPS = 2
RECV = 8
EDGE = 16
CHUNK = 8
STRIP = 48
LANES = 128


TAU = 0.05
SIGMA_AXIAL = 1.5
SIGMA_RADIAL = 4.0
MESH = pl.DeviceIdType.MESH


def sweep_plane(med, src, dst, prev, x, count):
    ahead = jnp.minimum(x + 1, count - 1)
    inside = jnp.where(x + 1 < count, TAU, 0.0)
    now, last = lax.rem(x, 2), 1 - lax.rem(x, 2)
    rows, cols = src.shape[2:]
    for start in range(0, rows, STRIP):
        part = pl.ds(start, STRIP)
        viscous = TAU * med[0, x, part].astype(jnp.float32)
        for c in range(2):
            prev[now, c, pl.ds(8 + start, STRIP)] = viscous * src[c, x, part]
    col = lax.broadcasted_iota(jnp.int32, (STRIP, cols), 1)
    for start in range(0, rows, STRIP):
        part = pl.ds(start, STRIP)
        scaled = TAU * med[2, x, part].astype(jnp.float32)
        coupling = TAU * med[3, x, part].astype(jnp.float32)
        pull = med[0, ahead, part].astype(jnp.float32) + med[1, ahead, part].astype(jnp.float32)
        pull = pull * inside
        keep = 1.0 - (6.0 * TAU) * med[0, x, part].astype(jnp.float32)
        keep = keep - (TAU * med[1, x, part].astype(jnp.float32) + scaled)
        values = src[0, x, part], src[1, x, part]
        for c in range(2):
            flux = prev[now, c, pl.ds(8 + start, STRIP)]
            total = prev[last, c, pl.ds(8 + start, STRIP)] + pull * src[c, ahead, part]
            total = total + jnp.where(col == 0, 0.0, pltpu.roll(flux, 1, 1))
            total = total + jnp.where(col == cols - 1, 0.0, pltpu.roll(flux, cols - 1, 1))
            total = total + prev[now, c, pl.ds(7 + start, STRIP)]
            total = total + prev[now, c, pl.ds(9 + start, STRIP)]
            if c == 0:
                total = total + TAU * med[4, x, part].astype(jnp.float32)
                dst[0, x, part] = keep * values[0] - coupling * values[1] + total
            else:
                dst[1, x, part] = (keep - scaled) * values[1] - coupling * values[0] + total


def pack_tables(me, rotors, listed, moved, target, pack):
    turb_dev, slots, moved_dev = rotors.shape[1], listed.shape[1], moved.shape[0]
    pack[...] = jnp.full(pack.shape, -1.0, jnp.float32)
    own = pl.ds(0, turb_dev)
    pack[0:2, own] = rotors[0:2]
    pack[2:3, own] = jnp.cos(rotors[2:3])
    pack[3:4, own] = jnp.sin(rotors[2:3])
    pack[4:5, own] = rotors[3:4]
    for group in range(-(-slots // LANES)):
        size = min(LANES, slots - group * LANES)
        pack[5 + group : 6 + group, pl.ds(0, size)] = listed[
            :, pl.ds(group * LANES, size)
        ].astype(jnp.float32)
    full = pack[...]
    lane = lax.broadcasted_iota(jnp.int32, full.shape, 1)
    field = lax.broadcasted_iota(jnp.int32, full.shape, 0) + 2
    line = jnp.full((1, LANES), -1.0, jnp.float32)
    for j in range(moved_dev):
        picked = jnp.sum(jnp.where(lane == moved[j], full, 0.0), axis=1, keepdims=True)
        here = (lane == moved_dev * field + j) & (field < 7)
        spread = jnp.sum(jnp.where(here, picked, 0.0), axis=0, keepdims=True)
        place = lane[0:1]
        for f in range(2, 7):
            line = jnp.where(place == moved_dev * f + j, spread, line)
        line = jnp.where(place == j, target[j, 0].astype(jnp.float32), line)
        number = (me * turb_dev + moved[j]).astype(jnp.float32)
        line = jnp.where(place == moved_dev + j, number, line)
    pack[7:8] = line


def relax_kernel(
    sizes,
    rotors,
    listed,
    moved,
    target,
    q_hbm,
    med_hbm,
    out_hbm,
    every,
    q,
    med,
    q1,
    prev,
    xs,
    xr,
    ys,
    yr,
    pack,
    table,
    edge_sem,
    in_sem,
    out_sem,
    ssem,
    rsem,
    tsend,
    trecv,
):
    n_gx, n_gy = sizes
    n = n_gx * n_gy
    _, count, width, _ = q.shape
    chunks = count // CHUNK
    gx, gy = lax.axis_index("gx"), lax.axis_index("gy")
    x_lo, x_hi = lax.rem(gx + n_gx - 1, n_gx), lax.rem(gx + 1, n_gx)
    y_lo, y_hi = lax.rem(gy + n_gy - 1, n_gy), lax.rem(gy + 1, n_gy)
    peers = ((x_lo, gy), (x_hi, gy), (gx, y_lo), (gx, y_hi))
    mid = pl.ds(EDGE, width - 2 * EDGE)
    edges = (pl.ds(0, EDGE), pl.ds(width - EDGE, EDGE))

    edge_in = []
    for i, part in enumerate(edges):
        edge_in.append(pltpu.make_async_copy(q_hbm.at[:, :, part], q.at[:, :, part], edge_sem.at[i, 0]))
        edge_in.append(
            pltpu.make_async_copy(med_hbm.at[0, :, part], med.at[0, :, part], edge_sem.at[i, 1])
        )

    def chunk_in(i):
        part = pl.ds(i * CHUNK, CHUNK)
        return (
            pltpu.make_async_copy(q_hbm.at[:, part, mid], q.at[:, part, mid], in_sem.at[i, 0]),
            pltpu.make_async_copy(med_hbm.at[0, part, mid], med.at[0, part, mid], in_sem.at[i, 1]),
            pltpu.make_async_copy(
                med_hbm.at[pl.ds(1, 4), part], med.at[pl.ds(1, 4), part], in_sem.at[i, 2]
            ),
        )

    for copy in edge_in:
        copy.start()
    for i in [0, chunks - 1] + list(range(1, chunks - 1)):
        for copy in chunk_in(i):
            copy.start()

    barrier = pltpu.get_barrier_semaphore()
    me = gx * n_gy + gy

    @pl.loop(1, n)
    def _(i):
        other = lax.rem(me + i, n)
        pl.semaphore_signal(
            barrier,
            inc=1,
            device_id=(lax.div(other, n_gy), lax.rem(other, n_gy)),
            device_id_type=MESH,
        )

    pack_tables(me, rotors, listed, moved, target, pack)
    pl.semaphore_wait(barrier, n - 1)

    def share(i, place):
        other = lax.rem(me + i, n)
        return pltpu.make_async_remote_copy(
            src_ref=pack,
            dst_ref=table.at[place],
            send_sem=tsend.at[i],
            recv_sem=trecv.at[place],
            device_id=(lax.div(other, n_gy), lax.rem(other, n_gy)),
            device_id_type=MESH,
        )

    def exchange(turn, src):
        for c in range(2):
            low, high = med[0, 0].astype(jnp.float32), med[0, count - 1].astype(jnp.float32)
            xs[turn, 0, c] = (low + med[1, 0].astype(jnp.float32)) * src[c, 0]
            xs[turn, 1, c] = high * src[c, count - 1]

        copies = []
        for side in range(2):
            copies.append(
                pltpu.make_async_remote_copy(
                    src_ref=xs.at[turn, side],
                    dst_ref=xr.at[turn, side],
                    send_sem=ssem.at[turn, side],
                    recv_sem=rsem.at[turn, side],
                    device_id=peers[side],
                    device_id_type=MESH,
                )
            )
            copies[-1].start()

        @pl.loop(0, count, unroll=4)
        def _(x):
            low = med[0, x, pl.ds(0, EDGE)].astype(jnp.float32)[:8]
            high = med[0, x, pl.ds(width - EDGE, EDGE)].astype(jnp.float32)[8:]
            for c in range(2):
                ys[turn, 0, c, pl.ds(x, 1)] = (low * src[c, x, pl.ds(0, 8)])[:1]
                ys[turn, 1, c, pl.ds(x, 1)] = (high * src[c, x, pl.ds(width - 8, 8)])[7:]

        for side in range(2):
            copies.append(
                pltpu.make_async_remote_copy(
                    src_ref=ys.at[turn, side],
                    dst_ref=yr.at[turn, side],
                    send_sem=ssem.at[turn, 2 + side],
                    recv_sem=rsem.at[turn, 2 + side],
                    device_id=peers[2 + side],
                    device_id_type=MESH,
                )
            )
            copies[-1].start()
        return copies

    def patch(turn, dst):
        has_hi_x = jnp.where(gx < n_gx - 1, TAU, 0.0)
        has_lo_x = jnp.where(gx > 0, TAU, 0.0)
        has_hi_y = jnp.where(gy < n_gy - 1, TAU, 0.0)
        has_lo_y = jnp.where(gy > 0, TAU, 0.0)
        for c in range(2):
            dst[c, count - 1] = dst[c, count - 1] + has_hi_x * xr[turn, 0, c]
            dst[c, 0] = dst[c, 0] + has_lo_x * xr[turn, 1, c]

        @pl.loop(0, count, unroll=4)
        def _(x):
            for c in range(2):
                last = pl.ds(width - 1, 1)
                first = pl.ds(0, 1)
                dst[c, x, last] = dst[c, x, last] + has_hi_y * yr[turn, 0, c, pl.ds(x, 1)]
                dst[c, x, first] = dst[c, x, first] + has_lo_y * yr[turn, 1, c, pl.ds(x, 1)]

    for copy in edge_in:
        copy.wait()
    for i in (0, chunks - 1):
        for copy in chunk_in(i):
            copy.wait()

    copies = exchange(0, q)

    @pl.loop(1, n)
    def _(i):
        share(i, me).start()

    table[me] = pack[...]
    prev[...] = jnp.zeros_like(prev)
    for i in range(chunks):
        if 0 < i + 1 < chunks - 1:
            for copy in chunk_in(i + 1):
                copy.wait()

        @pl.loop(0, CHUNK, unroll=2)
        def _(j):
            sweep_plane(med, q, q1, prev, i * CHUNK + j, count)

    for copy in copies:
        copy.wait()
    patch(0, q1)

    copies = exchange(1, q1)
    prev[...] = jnp.zeros_like(prev)

    def chunk_out(i):
        part = pl.ds(i * CHUNK, CHUNK)
        return pltpu.make_async_copy(q.at[:, part, mid], out_hbm.at[:, part, mid], out_sem.at[i])

    outs = []
    for i in range(chunks):

        @pl.loop(0, CHUNK, unroll=2)
        def _(j):
            sweep_plane(med, q1, q, prev, i * CHUNK + j, count)

        if 0 < i < chunks - 1:
            outs.append(chunk_out(i))
            outs[-1].start()

    @pl.loop(1, n)
    def _(i):
        share(i, me).wait_send()
        share(i, lax.rem(me + i, n)).wait_recv()

    every[...] = table[...]
    for copy in copies:
        copy.wait()
    patch(1, q)
    tail = [chunk_out(0), chunk_out(chunks - 1)]
    for i, part in enumerate(edges):
        sem = out_sem.at[chunks + i]
        tail.append(pltpu.make_async_copy(q.at[:, :, part], out_hbm.at[:, :, part], sem))
    for copy in tail:
        copy.start()
    for copy in outs + tail:
        copy.wait()


def relax(adjoint, medium, rotors, slot_turbine, moved_rotors, new_brick, sizes):
    n = sizes[0] * sizes[1]
    vmem, smem = pl.BlockSpec(memory_space=pltpu.VMEM), pl.BlockSpec(memory_space=pltpu.SMEM)
    channels, count, width, depth = adjoint.shape
    return pl.pallas_call(
        functools.partial(relax_kernel, sizes),
        out_shape=(
            jax.ShapeDtypeStruct(adjoint.shape, jnp.float32),
            jax.ShapeDtypeStruct((n, 8, LANES), jnp.float32),
        ),
        in_specs=[vmem, vmem, smem, smem] + [pl.BlockSpec(memory_space=pl.ANY)] * 2,
        out_specs=(pl.BlockSpec(memory_space=pl.ANY), vmem),
        scratch_shapes=[
            pltpu.VMEM(adjoint.shape, jnp.float32),
            pltpu.VMEM(medium.shape, jnp.bfloat16),
            pltpu.VMEM(adjoint.shape, jnp.float32),
            pltpu.VMEM((2, channels, width + 16, depth), jnp.float32),
            pltpu.VMEM((2, 2, channels, width, depth), jnp.float32),
            pltpu.VMEM((2, 2, channels, width, depth), jnp.float32),
            pltpu.VMEM((2, 2, channels, count, depth), jnp.float32),
            pltpu.VMEM((2, 2, channels, count, depth), jnp.float32),
            pltpu.VMEM((8, LANES), jnp.float32),
            pltpu.VMEM((n, 8, LANES), jnp.float32),
            pltpu.SemaphoreType.DMA((2, 2)),
            pltpu.SemaphoreType.DMA((count // CHUNK, 3)),
            pltpu.SemaphoreType.DMA((2 + count // CHUNK,)),
            pltpu.SemaphoreType.DMA((2, 4)),
            pltpu.SemaphoreType.DMA((2, 4)),
            pltpu.SemaphoreType.DMA((n,)),
            pltpu.SemaphoreType.DMA((n,)),
        ],
        compiler_params=pltpu.CompilerParams(
            collective_id=0, has_side_effects=True, vmem_limit_bytes=48 * 1024 * 1024
        ),
        name="relax",
    )(rotors, slot_turbine[None, :], moved_rotors, new_brick, adjoint, medium)


def z_weights(depth):
    z = np.arange(depth)[:, None] - np.arange(depth)[None, :]
    height = z + 0.5 - KZ / 2.0
    values = np.exp(-(height**2) / (2.0 * SIGMA_RADIAL**2)) * ((z >= 0) & (z < KZ))
    values = values.T.astype(np.float32)
    high = values.astype(jnp.bfloat16)
    low = (values - high.astype(np.float32)).astype(jnp.bfloat16)
    return np.block([[high, high], [low, np.zeros_like(low)]])


def slope_kernel(
    turb_dev,
    slot_turbine,
    corner,
    table_hbm,
    q_hbm,
    profile,
    out_hbm,
    slopes,
    q,
    conv,
    sums,
    table,
    table_sem,
    in_sem,
    out_sem,
):
    _, count, width, depth = q.shape
    chunks = count // CHUNK
    slots = slot_turbine.shape[0]

    def chunk_in(i):
        part = pl.ds(i * CHUNK, CHUNK)
        return pltpu.make_async_copy(q_hbm.at[:, part], q.at[:, part], in_sem.at[i])

    def chunk_out(i):
        part = pl.ds(i * CHUNK, CHUNK)
        return pltpu.make_async_copy(q.at[:, part], out_hbm.at[:, part], out_sem.at[i])

    fetch = pltpu.make_async_copy(table_hbm, table, table_sem)
    fetch.start()
    for i in range(chunks):
        chunk_in(i).start()
    for i in range(chunks):
        chunk_in(i).wait()
        chunk_out(i).start()

        @pl.loop(0, CHUNK, unroll=4)
        def _(j):
            x = i * CHUNK + j
            plane = q[0, x]
            high = plane.astype(jnp.bfloat16)
            low = (plane - high.astype(jnp.float32)).astype(jnp.bfloat16)
            both = lax.dot_general(
                profile[...],
                jnp.concatenate([high, low], axis=1),
                (((1,), (1,)), ((), ())),
                preferred_element_type=jnp.float32,
            )
            conv[pl.ds(x * depth, depth), pl.ds(0, width)] = both[:depth] + both[depth:]

    fetch.wait()
    slopes[...] = jnp.zeros_like(slopes)
    groups = -(-slots // LANES)
    shape = (KX, LANES)
    lane = lax.broadcasted_iota(jnp.int32, shape, 1)
    cell_x = lax.broadcasted_iota(jnp.int32, shape, 0).astype(jnp.float32) + 0.5 - KX / 2.0
    cell_y = lax.rem(lane, KY).astype(jnp.float32) + 0.5 - KY / 2.0
    share = LANES // KY
    part = lax.div(lane, KY)

    def line_of_slots(line, carry):
        values = jnp.zeros(shape, jnp.float32)
        fields = [jnp.zeros(shape, jnp.float32)] * 5
        for j in range(share):
            s = line * share + j
            turbine = jnp.maximum(slot_turbine[s], 0)
            first_x = jnp.minimum(corner[0, s], count - KX)
            first_y = jnp.minimum(corner[1, s], width - KY)
            first_z = jnp.minimum(corner[2, s], depth - KZ)
            block = conv[pl.ds(first_x * depth + first_z, KX, depth), :]
            block = pltpu.roll(block, lax.rem(j * KY - first_y + LANES, LANES), 1)
            mine = part == j
            values = jnp.where(mine, block, values)
            owner, local = lax.div(turbine, turb_dev), lax.rem(turbine, turb_dev)
            fields = [
                jnp.where(mine, table[owner, i, local], old) for i, old in enumerate(fields)
            ]
        sub_x, sub_y, cosine, sine, thrust = fields
        delta_x, delta_y = cell_x - sub_x, cell_y - sub_y
        along = cosine * delta_x + sine * delta_y
        across = cosine * delta_y - sine * delta_x
        kernel = thrust * jnp.exp(
            -along * along / (2.0 * SIGMA_AXIAL * SIGMA_AXIAL)
            - across * across / (2.0 * SIGMA_RADIAL * SIGMA_RADIAL)
        )
        weighted = kernel * values
        axial = along * (1.0 / (SIGMA_AXIAL * SIGMA_AXIAL))
        radial = across * (1.0 / (SIGMA_RADIAL * SIGMA_RADIAL))
        sums[0, pl.ds(line, 1)] = jnp.sum(
            weighted * (axial * cosine - radial * sine), axis=0, keepdims=True
        )
        sums[1, pl.ds(line, 1)] = jnp.sum(
            weighted * (axial * sine + radial * cosine), axis=0, keepdims=True
        )
        return carry

    sums[...] = jnp.zeros_like(sums)
    lax.fori_loop(0, slots // share, line_of_slots, 0, unroll=2)
    spread = lax.div(lax.broadcasted_iota(jnp.int32, (LANES, LANES), 0), KY) == lax.rem(
        lax.broadcasted_iota(jnp.int32, (LANES, LANES), 1), share
    )
    spread = jnp.where(spread, 1.0, 0.0)
    lines = LANES // share
    own = lax.div(lax.broadcasted_iota(jnp.int32, (lines, LANES), 1), share)
    own = own == lax.broadcasted_iota(jnp.int32, (lines, LANES), 0)
    for i in range(2):
        total = jnp.dot(
            sums[i],
            spread,
            precision=lax.Precision.HIGHEST,
            preferred_element_type=jnp.float32,
        )
        for group in range(groups):
            block = total[group * lines : (group + 1) * lines]
            row = i * groups + group
            slopes[row : row + 1] = jnp.sum(jnp.where(own, block, 0.0), axis=0, keepdims=True)
    for i in range(chunks):
        chunk_out(i).wait()


def slot_slopes(state, slot_turbine, slot_corner, table, turb_dev):
    _, count, width, depth = state.shape
    smem = pl.BlockSpec(memory_space=pltpu.SMEM)
    return pl.pallas_call(
        functools.partial(slope_kernel, turb_dev),
        out_shape=(
            jax.ShapeDtypeStruct(state.shape, jnp.float32),
            jax.ShapeDtypeStruct((8, LANES), jnp.float32),
        ),
        in_specs=[
            smem,
            smem,
            pl.BlockSpec(memory_space=pl.ANY),
            pl.BlockSpec(memory_space=pl.ANY),
            pl.BlockSpec(memory_space=pltpu.VMEM),
        ],
        out_specs=(
            pl.BlockSpec(memory_space=pl.ANY),
            pl.BlockSpec(memory_space=pltpu.VMEM),
        ),
        scratch_shapes=[
            pltpu.VMEM(state.shape, jnp.float32),
            pltpu.VMEM((count * depth, LANES), jnp.float32),
            pltpu.VMEM((2, -(-slot_turbine.shape[0] // LANES) * KY, LANES), jnp.float32),
            pltpu.SMEM(table.shape, jnp.float32),
            pltpu.SemaphoreType.DMA,
            pltpu.SemaphoreType.DMA((count // CHUNK,)),
            pltpu.SemaphoreType.DMA((count // CHUNK,)),
        ],
        compiler_params=pltpu.CompilerParams(vmem_limit_bytes=58 * 1024 * 1024),
        name="slopes",
    )(slot_turbine, slot_corner, table, state, jnp.asarray(z_weights(depth)))


def share_kernel(sizes, slopes, out, every, ssem, rsem):
    n_gx, n_gy = sizes
    n = n_gx * n_gy
    gx, gy = lax.axis_index("gx"), lax.axis_index("gy")
    me = gx * n_gy + gy
    barrier = pltpu.get_barrier_semaphore()

    def peer(i):
        other = lax.rem(me + i, n)
        return (lax.div(other, n_gy), lax.rem(other, n_gy))

    @pl.loop(1, n)
    def _(i):
        pl.semaphore_signal(barrier, inc=1, device_id=peer(i), device_id_type=MESH)

    pl.semaphore_wait(barrier, n - 1)

    def send(i):
        return pltpu.make_async_remote_copy(
            src_ref=slopes,
            dst_ref=every.at[me],
            send_sem=ssem.at[i],
            recv_sem=rsem.at[me],
            device_id=peer(i),
            device_id_type=MESH,
        )

    @pl.loop(1, n)
    def _(i):
        send(i).start()

    every[me] = slopes[...]

    @pl.loop(1, n)
    def _(i):
        send(i).wait_send()
        other = lax.rem(me + i, n)
        pltpu.make_async_remote_copy(
            src_ref=slopes,
            dst_ref=every.at[other],
            send_sem=ssem.at[i],
            recv_sem=rsem.at[other],
            device_id=peer(i),
            device_id_type=MESH,
        ).wait_recv()

    out[...] = every[...]


def finish_kernel(sizes, groups, moved_dev, step_size, every, table, step_out, incoming):
    n = sizes[0] * sizes[1]
    me = lax.axis_index("gx") * sizes[1] + lax.axis_index("gy")
    turb_dev = step_out.shape[1]

    lines = table[:, 7]
    lane = lax.broadcasted_iota(jnp.int32, lines.shape, 1)
    mine = jnp.where((lines == me.astype(jnp.float32)) & (lane < moved_dev), 1.0, 0.0)

    def earlier(size, row, col):
        less = lax.broadcasted_iota(jnp.int32, (size, size), row) < lax.broadcasted_iota(
            jnp.int32, (size, size), col
        )
        return jnp.where(less, 1.0, 0.0).astype(jnp.bfloat16)

    rank = jnp.sum(
        jnp.dot(
            earlier(n, 1, 0), mine.astype(jnp.bfloat16), preferred_element_type=jnp.float32
        ),
        axis=1,
        keepdims=True,
    ) + jnp.dot(
        mine.astype(jnp.bfloat16), earlier(LANES, 0, 1), preferred_element_type=jnp.float32
    )
    shifted = [pltpu.roll(lines, LANES - moved_dev * f, 1) for f in range(1, 7)]
    chosen = [jnp.where(rank == float(slot), mine, 0.0) for slot in range(RECV)]

    def per_slot(values):
        parts = [jnp.sum(pick * values, axis=0, keepdims=True) for pick in chosen]
        return jnp.sum(jnp.concatenate(parts, axis=0), axis=1, keepdims=True)

    valid = per_slot(jnp.ones_like(lines))
    wanted, sub_x, sub_y, cosine, sine, thrust = [per_slot(values) for values in shifted]
    own = (
        me * turb_dev + lax.broadcasted_iota(jnp.int32, (turb_dev, LANES), 0)
    ).astype(jnp.float32)
    targets = jnp.concatenate([own, jnp.broadcast_to(wanted, (RECV, LANES))], axis=0)

    def collect(d, carry):
        sum_x, sum_y = carry
        for group in range(groups):
            hit = targets == table[d, pl.ds(5 + group, 1)]
            sum_x = sum_x + jnp.where(hit, every[d, pl.ds(group, 1)], 0.0)
            sum_y = sum_y + jnp.where(hit, every[d, pl.ds(groups + group, 1)], 0.0)
        return sum_x, sum_y

    zero = jnp.zeros((turb_dev + RECV, LANES), jnp.float32)
    sums = lax.fori_loop(0, n, collect, (zero, zero), unroll=2)
    step = step_size[0]
    taken = [
        jnp.clip(-step * jnp.sum(part, axis=1, keepdims=True), -0.5, 0.5) for part in sums
    ]
    flip = lax.broadcasted_iota(jnp.int32, (turb_dev, turb_dev), 0) == lax.broadcasted_iota(
        jnp.int32, (turb_dev, turb_dev), 1
    )
    for i in range(2):
        step_out[i : i + 1] = jnp.sum(
            jnp.where(flip, taken[i][:turb_dev], 0.0), axis=0, keepdims=True
        )
    cells = KX * KY * KZ
    cell = lax.broadcasted_iota(jnp.int32, (RECV, cells), 1)
    ex = (cell // (KY * KZ)).astype(jnp.float32) + 0.5 - KX / 2.0
    ey = lax.rem(cell // KZ, KY).astype(jnp.float32) + 0.5 - KY / 2.0
    ez = lax.rem(cell, KZ).astype(jnp.float32) + 0.5 - KZ / 2.0
    delta_x = ex - (sub_x + taken[0][turb_dev:])
    delta_y = ey - (sub_y + taken[1][turb_dev:])
    along = cosine * delta_x + sine * delta_y
    across = cosine * delta_y - sine * delta_x
    kernel = thrust * jnp.exp(
        -along * along / (2.0 * SIGMA_AXIAL * SIGMA_AXIAL)
        - (across * across + ez * ez) / (2.0 * SIGMA_RADIAL * SIGMA_RADIAL)
    )
    incoming[...] = jnp.where(valid > 0, kernel, 0.0).astype(jnp.bfloat16)


def finish(step_size, slopes, table, turb_dev, groups, moved_dev, sizes):
    n = sizes[0] * sizes[1]
    vmem = pl.BlockSpec(memory_space=pltpu.VMEM)

    every = pl.pallas_call(
        functools.partial(share_kernel, sizes),
        out_shape=jax.ShapeDtypeStruct((n,) + slopes.shape, jnp.float32),
        in_specs=[vmem],
        out_specs=vmem,
        scratch_shapes=[
            pltpu.VMEM((n,) + slopes.shape, jnp.float32),
            pltpu.SemaphoreType.DMA((n,)),
            pltpu.SemaphoreType.DMA((n,)),
        ],
        compiler_params=pltpu.CompilerParams(collective_id=1, has_side_effects=True),
        name="share",
    )(slopes)
    return pl.pallas_call(
        functools.partial(finish_kernel, sizes, groups, moved_dev),
        out_shape=(
            jax.ShapeDtypeStruct((2, turb_dev), jnp.float32),
            jax.ShapeDtypeStruct((RECV, KX * KY * KZ), jnp.bfloat16),
        ),
        in_specs=[pl.BlockSpec(memory_space=pltpu.SMEM), vmem, vmem],
        out_specs=(vmem, vmem),
        name="finish",
    )(step_size, every, table)


def body(
    sizes, adjoint, medium, rotors, step_size, slot_turbine, slot_corner, moved_rotors, new_brick
):
    turb_dev = rotors.shape[1]
    groups = -(-slot_turbine.shape[0] // LANES)
    state, table = relax(adjoint, medium, rotors, slot_turbine, moved_rotors, new_brick, sizes)
    state, slopes = slot_slopes(state, slot_turbine, slot_corner, table, turb_dev)
    step_taken, incoming = finish(
        step_size.reshape(1), slopes, table, turb_dev, groups, moved_rotors.shape[0], sizes
    )
    return (state, step_taken, incoming)


def solution(mesh):
    sizes = (mesh.shape["gx"], mesh.shape["gy"])
    return jax.shard_map(
        functools.partial(body, sizes),
        mesh=mesh,
        in_specs=(
            P(None, "gx", "gy", None),
            P(None, "gx", "gy", None),
            P(None, ("gx", "gy")),
            P(),
            P(("gx", "gy")),
            P(None, ("gx", "gy")),
            P(("gx", "gy")),
            P(("gx", "gy"), None),
        ),
        out_specs=(P(None, "gx", "gy", None), P(None, ("gx", "gy")), P(("gx", "gy"), None)),
        check_vma=False,
    )
```

```python
import functools

import jax
import jax.numpy as jnp
import numpy as np
from jax import lax
from jax.experimental import pallas as pl
from jax.experimental.pallas import tpu as pltpu
from jax.sharding import PartitionSpec as P

KX = 8
KY = 16
KZ = 16
SWEEPS = 2
RECV = 8
EDGE = 16
CHUNK = 8
STRIP = 48
LANES = 128


TAU = 0.05
SIGMA_AXIAL = 1.5
SIGMA_RADIAL = 4.0
MESH = pl.DeviceIdType.MESH


def sweep_plane(med, src, dst, prev, x, count):
    ahead = jnp.minimum(x + 1, count - 1)
    inside = jnp.where(x + 1 < count, TAU, 0.0)
    now, last = lax.rem(x, 2), 1 - lax.rem(x, 2)
    rows, cols = src.shape[2:]
    for start in range(0, rows, STRIP):
        part = pl.ds(start, STRIP)
        viscous = TAU * med[0, x, part].astype(jnp.float32)
        for c in range(2):
            prev[now, c, pl.ds(8 + start, STRIP)] = viscous * src[c, x, part]
    col = lax.broadcasted_iota(jnp.int32, (STRIP, cols), 1)
    for start in range(0, rows, STRIP):
        part = pl.ds(start, STRIP)
        scaled = TAU * med[2, x, part].astype(jnp.float32)
        coupling = TAU * med[3, x, part].astype(jnp.float32)
        pull = med[0, ahead, part].astype(jnp.float32) + med[1, ahead, part].astype(jnp.float32)
        pull = pull * inside
        keep = 1.0 - (6.0 * TAU) * med[0, x, part].astype(jnp.float32)
        keep = keep - (TAU * med[1, x, part].astype(jnp.float32) + scaled)
        values = src[0, x, part], src[1, x, part]
        for c in range(2):
            flux = prev[now, c, pl.ds(8 + start, STRIP)]
            total = prev[last, c, pl.ds(8 + start, STRIP)] + pull * src[c, ahead, part]
            total = total + jnp.where(col == 0, 0.0, pltpu.roll(flux, 1, 1))
            total = total + jnp.where(col == cols - 1, 0.0, pltpu.roll(flux, cols - 1, 1))
            total = total + prev[now, c, pl.ds(7 + start, STRIP)]
            total = total + prev[now, c, pl.ds(9 + start, STRIP)]
            if c == 0:
                total = total + TAU * med[4, x, part].astype(jnp.float32)
                dst[0, x, part] = keep * values[0] - coupling * values[1] + total
            else:
                dst[1, x, part] = (keep - scaled) * values[1] - coupling * values[0] + total


def pack_tables(me, rotors, listed, moved, target, pack):
    turb_dev, slots, moved_dev = rotors.shape[1], listed.shape[1], moved.shape[0]
    pack[...] = jnp.full(pack.shape, -1.0, jnp.float32)
    own = pl.ds(0, turb_dev)
    pack[0:2, own] = rotors[0:2]
    pack[2:3, own] = jnp.cos(rotors[2:3])
    pack[3:4, own] = jnp.sin(rotors[2:3])
    pack[4:5, own] = rotors[3:4]
    for group in range(-(-slots // LANES)):
        size = min(LANES, slots - group * LANES)
        pack[5 + group : 6 + group, pl.ds(0, size)] = listed[
            :, pl.ds(group * LANES, size)
        ].astype(jnp.float32)
    full = pack[...]
    lane = lax.broadcasted_iota(jnp.int32, full.shape, 1)
    field = lax.broadcasted_iota(jnp.int32, full.shape, 0) + 2
    line = jnp.full((1, LANES), -1.0, jnp.float32)
    for j in range(moved_dev):
        picked = jnp.sum(jnp.where(lane == moved[j], full, 0.0), axis=1, keepdims=True)
        here = (lane == moved_dev * field + j) & (field < 7)
        spread = jnp.sum(jnp.where(here, picked, 0.0), axis=0, keepdims=True)
        place = lane[0:1]
        for f in range(2, 7):
            line = jnp.where(place == moved_dev * f + j, spread, line)
        line = jnp.where(place == j, target[j, 0].astype(jnp.float32), line)
        number = (me * turb_dev + moved[j]).astype(jnp.float32)
        line = jnp.where(place == moved_dev + j, number, line)
    pack[7:8] = line


def greet(sizes):
    n_gx, n_gy = sizes
    gx, gy = lax.axis_index("gx"), lax.axis_index("gy")
    barrier = pltpu.get_barrier_semaphore()
    for j in range(1, n_gy):
        pl.semaphore_signal(
            barrier, inc=1, device_id=(gx, lax.rem(gy + j, n_gy)), device_id_type=MESH
        )
    for j in range(1, n_gx):
        pl.semaphore_signal(
            barrier, inc=1, device_id=(lax.rem(gx + j, n_gx), gy), device_id_type=MESH
        )
    return n_gx + n_gy - 2


def spread_y(sizes, own, every, ssem, rsem):
    n_gy = sizes[1]
    gx, gy = lax.axis_index("gx"), lax.axis_index("gy")
    return [
        pltpu.make_async_remote_copy(
            src_ref=own,
            dst_ref=every.at[gx * n_gy + gy],
            send_sem=ssem.at[j],
            recv_sem=rsem.at[j],
            device_id=(gx, lax.rem(gy + j, n_gy)),
            device_id_type=MESH,
        )
        for j in range(1, n_gy)
    ]


def spread_x(sizes, every, ssem, rsem):
    n_gx, n_gy = sizes
    gx, gy = lax.axis_index("gx"), lax.axis_index("gy")
    block = every.at[pl.ds(gx * n_gy, n_gy)]
    return [
        pltpu.make_async_remote_copy(
            src_ref=block,
            dst_ref=block,
            send_sem=ssem.at[n_gy + j],
            recv_sem=rsem.at[n_gy + j],
            device_id=(lax.rem(gx + j, n_gx), gy),
            device_id_type=MESH,
        )
        for j in range(1, n_gx)
    ]


def relax_kernel(
    sizes,
    rotors,
    listed,
    moved,
    target,
    q_hbm,
    med_hbm,
    out_hbm,
    every,
    q,
    med,
    q1,
    prev,
    xs,
    xr,
    ys,
    yr,
    pack,
    table,
    edge_sem,
    in_sem,
    out_sem,
    ssem,
    rsem,
    tsend,
    trecv,
):
    n_gx, n_gy = sizes
    _, count, width, _ = q.shape
    chunks = count // CHUNK
    gx, gy = lax.axis_index("gx"), lax.axis_index("gy")
    x_lo, x_hi = lax.rem(gx + n_gx - 1, n_gx), lax.rem(gx + 1, n_gx)
    y_lo, y_hi = lax.rem(gy + n_gy - 1, n_gy), lax.rem(gy + 1, n_gy)
    peers = ((x_lo, gy), (x_hi, gy), (gx, y_lo), (gx, y_hi))
    mid = pl.ds(EDGE, width - 2 * EDGE)
    edges = (pl.ds(0, EDGE), pl.ds(width - EDGE, EDGE))

    edge_in = []
    for i, part in enumerate(edges):
        edge_in.append(pltpu.make_async_copy(q_hbm.at[:, :, part], q.at[:, :, part], edge_sem.at[i, 0]))
        edge_in.append(
            pltpu.make_async_copy(med_hbm.at[0, :, part], med.at[0, :, part], edge_sem.at[i, 1])
        )

    def chunk_in(i):
        part = pl.ds(i * CHUNK, CHUNK)
        return (
            pltpu.make_async_copy(q_hbm.at[:, part, mid], q.at[:, part, mid], in_sem.at[i, 0]),
            pltpu.make_async_copy(med_hbm.at[0, part, mid], med.at[0, part, mid], in_sem.at[i, 1]),
            pltpu.make_async_copy(
                med_hbm.at[pl.ds(1, 4), part], med.at[pl.ds(1, 4), part], in_sem.at[i, 2]
            ),
        )

    for copy in edge_in:
        copy.start()
    for i in [0, chunks - 1] + list(range(1, chunks - 1)):
        for copy in chunk_in(i):
            copy.start()

    barrier = pltpu.get_barrier_semaphore()
    me = gx * n_gy + gy

    met = greet(sizes)
    pack_tables(me, rotors, listed, moved, target, pack)
    pl.semaphore_wait(barrier, met)

    def exchange(turn, src):
        for c in range(2):
            low, high = med[0, 0].astype(jnp.float32), med[0, count - 1].astype(jnp.float32)
            xs[turn, 0, c] = (low + med[1, 0].astype(jnp.float32)) * src[c, 0]
            xs[turn, 1, c] = high * src[c, count - 1]

        copies = []
        for side in range(2):
            copies.append(
                pltpu.make_async_remote_copy(
                    src_ref=xs.at[turn, side],
                    dst_ref=xr.at[turn, side],
                    send_sem=ssem.at[turn, side],
                    recv_sem=rsem.at[turn, side],
                    device_id=peers[side],
                    device_id_type=MESH,
                )
            )
            copies[-1].start()

        @pl.loop(0, count, unroll=4)
        def _(x):
            low = med[0, x, pl.ds(0, EDGE)].astype(jnp.float32)[:8]
            high = med[0, x, pl.ds(width - EDGE, EDGE)].astype(jnp.float32)[8:]
            for c in range(2):
                ys[turn, 0, c, pl.ds(x, 1)] = (low * src[c, x, pl.ds(0, 8)])[:1]
                ys[turn, 1, c, pl.ds(x, 1)] = (high * src[c, x, pl.ds(width - 8, 8)])[7:]

        for side in range(2):
            copies.append(
                pltpu.make_async_remote_copy(
                    src_ref=ys.at[turn, side],
                    dst_ref=yr.at[turn, side],
                    send_sem=ssem.at[turn, 2 + side],
                    recv_sem=rsem.at[turn, 2 + side],
                    device_id=peers[2 + side],
                    device_id_type=MESH,
                )
            )
            copies[-1].start()
        return copies

    def patch(turn, dst):
        has_hi_x = jnp.where(gx < n_gx - 1, TAU, 0.0)
        has_lo_x = jnp.where(gx > 0, TAU, 0.0)
        has_hi_y = jnp.where(gy < n_gy - 1, TAU, 0.0)
        has_lo_y = jnp.where(gy > 0, TAU, 0.0)
        for c in range(2):
            dst[c, count - 1] = dst[c, count - 1] + has_hi_x * xr[turn, 0, c]
            dst[c, 0] = dst[c, 0] + has_lo_x * xr[turn, 1, c]

        @pl.loop(0, count, unroll=4)
        def _(x):
            for c in range(2):
                last = pl.ds(width - 1, 1)
                first = pl.ds(0, 1)
                dst[c, x, last] = dst[c, x, last] + has_hi_y * yr[turn, 0, c, pl.ds(x, 1)]
                dst[c, x, first] = dst[c, x, first] + has_lo_y * yr[turn, 1, c, pl.ds(x, 1)]

    for copy in edge_in:
        copy.wait()
    for i in (0, chunks - 1):
        for copy in chunk_in(i):
            copy.wait()

    copies = exchange(0, q)

    table[me] = pack[...]
    along_y = spread_y(sizes, pack, table, tsend, trecv)
    for copy in along_y:
        copy.start()
    prev[...] = jnp.zeros_like(prev)
    for i in range(chunks):
        if 0 < i + 1 < chunks - 1:
            for copy in chunk_in(i + 1):
                copy.wait()

        @pl.loop(0, CHUNK, unroll=2)
        def _(j):
            sweep_plane(med, q, q1, prev, i * CHUNK + j, count)

    for copy in copies:
        copy.wait()
    patch(0, q1)

    copies = exchange(1, q1)
    for copy in along_y:
        copy.wait()
    along_x = spread_x(sizes, table, tsend, trecv)
    for copy in along_x:
        copy.start()
    prev[...] = jnp.zeros_like(prev)

    def chunk_out(i):
        part = pl.ds(i * CHUNK, CHUNK)
        return pltpu.make_async_copy(q.at[:, part, mid], out_hbm.at[:, part, mid], out_sem.at[i])

    outs = []
    for i in range(chunks):

        @pl.loop(0, CHUNK, unroll=2)
        def _(j):
            sweep_plane(med, q1, q, prev, i * CHUNK + j, count)

        if 0 < i < chunks - 1:
            outs.append(chunk_out(i))
            outs[-1].start()

    for copy in along_x:
        copy.wait()
    every[...] = table[...]
    for copy in copies:
        copy.wait()
    patch(1, q)
    tail = [chunk_out(0), chunk_out(chunks - 1)]
    for i, part in enumerate(edges):
        sem = out_sem.at[chunks + i]
        tail.append(pltpu.make_async_copy(q.at[:, :, part], out_hbm.at[:, :, part], sem))
    for copy in tail:
        copy.start()
    for copy in outs + tail:
        copy.wait()


def relax(adjoint, medium, rotors, slot_turbine, moved_rotors, new_brick, sizes):
    n = sizes[0] * sizes[1]
    vmem, smem = pl.BlockSpec(memory_space=pltpu.VMEM), pl.BlockSpec(memory_space=pltpu.SMEM)
    channels, count, width, depth = adjoint.shape
    return pl.pallas_call(
        functools.partial(relax_kernel, sizes),
        out_shape=(
            jax.ShapeDtypeStruct(adjoint.shape, jnp.float32),
            jax.ShapeDtypeStruct((n, 8, LANES), jnp.float32),
        ),
        in_specs=[vmem, vmem, smem, smem] + [pl.BlockSpec(memory_space=pl.ANY)] * 2,
        out_specs=(pl.BlockSpec(memory_space=pl.ANY), vmem),
        scratch_shapes=[
            pltpu.VMEM(adjoint.shape, jnp.float32),
            pltpu.VMEM(medium.shape, jnp.bfloat16),
            pltpu.VMEM(adjoint.shape, jnp.float32),
            pltpu.VMEM((2, channels, width + 16, depth), jnp.float32),
            pltpu.VMEM((2, 2, channels, width, depth), jnp.float32),
            pltpu.VMEM((2, 2, channels, width, depth), jnp.float32),
            pltpu.VMEM((2, 2, channels, count, depth), jnp.float32),
            pltpu.VMEM((2, 2, channels, count, depth), jnp.float32),
            pltpu.VMEM((8, LANES), jnp.float32),
            pltpu.VMEM((n, 8, LANES), jnp.float32),
            pltpu.SemaphoreType.DMA((2, 2)),
            pltpu.SemaphoreType.DMA((count // CHUNK, 3)),
            pltpu.SemaphoreType.DMA((2 + count // CHUNK,)),
            pltpu.SemaphoreType.DMA((2, 4)),
            pltpu.SemaphoreType.DMA((2, 4)),
            pltpu.SemaphoreType.DMA((sizes[0] + sizes[1],)),
            pltpu.SemaphoreType.DMA((sizes[0] + sizes[1],)),
        ],
        compiler_params=pltpu.CompilerParams(
            collective_id=0, has_side_effects=True, vmem_limit_bytes=48 * 1024 * 1024
        ),
        name="relax",
    )(rotors, slot_turbine[None, :], moved_rotors, new_brick, adjoint, medium)


def z_weights(depth):
    z = np.arange(depth)[:, None] - np.arange(depth)[None, :]
    height = z + 0.5 - KZ / 2.0
    values = np.exp(-(height**2) / (2.0 * SIGMA_RADIAL**2)) * ((z >= 0) & (z < KZ))
    values = values.T.astype(np.float32)
    high = values.astype(jnp.bfloat16)
    low = (values - high.astype(np.float32)).astype(jnp.bfloat16)
    return np.block([[high, high], [low, np.zeros_like(low)]])


def slope_kernel(
    turb_dev,
    slot_turbine,
    corner,
    table_hbm,
    q_hbm,
    profile,
    out_hbm,
    slopes,
    q,
    conv,
    sums,
    table,
    table_sem,
    in_sem,
    out_sem,
):
    _, count, width, depth = q.shape
    chunks = count // CHUNK
    slots = slot_turbine.shape[0]

    def chunk_in(i):
        part = pl.ds(i * CHUNK, CHUNK)
        return pltpu.make_async_copy(q_hbm.at[:, part], q.at[:, part], in_sem.at[i])

    def chunk_out(i):
        part = pl.ds(i * CHUNK, CHUNK)
        return pltpu.make_async_copy(q.at[:, part], out_hbm.at[:, part], out_sem.at[i])

    fetch = pltpu.make_async_copy(table_hbm, table, table_sem)
    fetch.start()
    for i in range(chunks):
        chunk_in(i).start()
    for i in range(chunks):
        chunk_in(i).wait()
        chunk_out(i).start()

        @pl.loop(0, CHUNK, unroll=4)
        def _(j):
            x = i * CHUNK + j
            plane = q[0, x]
            high = plane.astype(jnp.bfloat16)
            low = (plane - high.astype(jnp.float32)).astype(jnp.bfloat16)
            both = lax.dot_general(
                profile[...],
                jnp.concatenate([high, low], axis=1),
                (((1,), (1,)), ((), ())),
                preferred_element_type=jnp.float32,
            )
            conv[pl.ds(x * depth, depth), pl.ds(0, width)] = both[:depth] + both[depth:]

    fetch.wait()
    slopes[...] = jnp.zeros_like(slopes)
    groups = -(-slots // LANES)
    shape = (KX, LANES)
    lane = lax.broadcasted_iota(jnp.int32, shape, 1)
    cell_x = lax.broadcasted_iota(jnp.int32, shape, 0).astype(jnp.float32) + 0.5 - KX / 2.0
    cell_y = lax.rem(lane, KY).astype(jnp.float32) + 0.5 - KY / 2.0
    share = LANES // KY
    part = lax.div(lane, KY)

    def line_of_slots(line, carry):
        values = jnp.zeros(shape, jnp.float32)
        fields = [jnp.zeros(shape, jnp.float32)] * 5
        for j in range(share):
            s = line * share + j
            turbine = jnp.maximum(slot_turbine[s], 0)
            first_x = jnp.minimum(corner[0, s], count - KX)
            first_y = jnp.minimum(corner[1, s], width - KY)
            first_z = jnp.minimum(corner[2, s], depth - KZ)
            block = conv[pl.ds(first_x * depth + first_z, KX, depth), :]
            block = pltpu.roll(block, lax.rem(j * KY - first_y + LANES, LANES), 1)
            mine = part == j
            values = jnp.where(mine, block, values)
            owner, local = lax.div(turbine, turb_dev), lax.rem(turbine, turb_dev)
            fields = [
                jnp.where(mine, table[owner, i, local], old) for i, old in enumerate(fields)
            ]
        sub_x, sub_y, cosine, sine, thrust = fields
        delta_x, delta_y = cell_x - sub_x, cell_y - sub_y
        along = cosine * delta_x + sine * delta_y
        across = cosine * delta_y - sine * delta_x
        kernel = thrust * jnp.exp(
            -along * along / (2.0 * SIGMA_AXIAL * SIGMA_AXIAL)
            - across * across / (2.0 * SIGMA_RADIAL * SIGMA_RADIAL)
        )
        weighted = kernel * values
        axial = along * (1.0 / (SIGMA_AXIAL * SIGMA_AXIAL))
        radial = across * (1.0 / (SIGMA_RADIAL * SIGMA_RADIAL))
        sums[0, pl.ds(line, 1)] = jnp.sum(
            weighted * (axial * cosine - radial * sine), axis=0, keepdims=True
        )
        sums[1, pl.ds(line, 1)] = jnp.sum(
            weighted * (axial * sine + radial * cosine), axis=0, keepdims=True
        )
        return carry

    sums[...] = jnp.zeros_like(sums)
    lax.fori_loop(0, slots // share, line_of_slots, 0, unroll=2)
    spread = lax.div(lax.broadcasted_iota(jnp.int32, (LANES, LANES), 0), KY) == lax.rem(
        lax.broadcasted_iota(jnp.int32, (LANES, LANES), 1), share
    )
    spread = jnp.where(spread, 1.0, 0.0)
    lines = LANES // share
    own = lax.div(lax.broadcasted_iota(jnp.int32, (lines, LANES), 1), share)
    own = own == lax.broadcasted_iota(jnp.int32, (lines, LANES), 0)
    for i in range(2):
        total = jnp.dot(
            sums[i],
            spread,
            precision=lax.Precision.HIGHEST,
            preferred_element_type=jnp.float32,
        )
        for group in range(groups):
            block = total[group * lines : (group + 1) * lines]
            row = i * groups + group
            slopes[row : row + 1] = jnp.sum(jnp.where(own, block, 0.0), axis=0, keepdims=True)
    for i in range(chunks):
        chunk_out(i).wait()


def slot_slopes(state, slot_turbine, slot_corner, table, turb_dev):
    _, count, width, depth = state.shape
    smem = pl.BlockSpec(memory_space=pltpu.SMEM)
    return pl.pallas_call(
        functools.partial(slope_kernel, turb_dev),
        out_shape=(
            jax.ShapeDtypeStruct(state.shape, jnp.float32),
            jax.ShapeDtypeStruct((8, LANES), jnp.float32),
        ),
        in_specs=[
            smem,
            smem,
            pl.BlockSpec(memory_space=pl.ANY),
            pl.BlockSpec(memory_space=pl.ANY),
            pl.BlockSpec(memory_space=pltpu.VMEM),
        ],
        out_specs=(
            pl.BlockSpec(memory_space=pl.ANY),
            pl.BlockSpec(memory_space=pltpu.VMEM),
        ),
        scratch_shapes=[
            pltpu.VMEM(state.shape, jnp.float32),
            pltpu.VMEM((count * depth, LANES), jnp.float32),
            pltpu.VMEM((2, -(-slot_turbine.shape[0] // LANES) * KY, LANES), jnp.float32),
            pltpu.SMEM(table.shape, jnp.float32),
            pltpu.SemaphoreType.DMA,
            pltpu.SemaphoreType.DMA((count // CHUNK,)),
            pltpu.SemaphoreType.DMA((count // CHUNK,)),
        ],
        compiler_params=pltpu.CompilerParams(vmem_limit_bytes=58 * 1024 * 1024),
        name="slopes",
    )(slot_turbine, slot_corner, table, state, jnp.asarray(z_weights(depth)))


def share_kernel(sizes, slopes, out, every, ssem, rsem):
    met = greet(sizes)
    every[lax.axis_index("gx") * sizes[1] + lax.axis_index("gy")] = slopes[...]
    pl.semaphore_wait(pltpu.get_barrier_semaphore(), met)
    along_y = spread_y(sizes, slopes, every, ssem, rsem)
    for copy in along_y:
        copy.start()
    for copy in along_y:
        copy.wait()
    along_x = spread_x(sizes, every, ssem, rsem)
    for copy in along_x:
        copy.start()
    for copy in along_x:
        copy.wait()
    out[...] = every[...]


def finish_kernel(sizes, groups, moved_dev, step_size, every, table, step_out, incoming):
    n = sizes[0] * sizes[1]
    me = lax.axis_index("gx") * sizes[1] + lax.axis_index("gy")
    turb_dev = step_out.shape[1]

    lines = table[:, 7]
    lane = lax.broadcasted_iota(jnp.int32, lines.shape, 1)
    mine = jnp.where((lines == me.astype(jnp.float32)) & (lane < moved_dev), 1.0, 0.0)

    def earlier(size, row, col):
        less = lax.broadcasted_iota(jnp.int32, (size, size), row) < lax.broadcasted_iota(
            jnp.int32, (size, size), col
        )
        return jnp.where(less, 1.0, 0.0).astype(jnp.bfloat16)

    rank = jnp.sum(
        jnp.dot(
            earlier(n, 1, 0), mine.astype(jnp.bfloat16), preferred_element_type=jnp.float32
        ),
        axis=1,
        keepdims=True,
    ) + jnp.dot(
        mine.astype(jnp.bfloat16), earlier(LANES, 0, 1), preferred_element_type=jnp.float32
    )
    shifted = [pltpu.roll(lines, LANES - moved_dev * f, 1) for f in range(1, 7)]
    chosen = [jnp.where(rank == float(slot), mine, 0.0) for slot in range(RECV)]

    def per_slot(values):
        parts = [jnp.sum(pick * values, axis=0, keepdims=True) for pick in chosen]
        return jnp.sum(jnp.concatenate(parts, axis=0), axis=1, keepdims=True)

    valid = per_slot(jnp.ones_like(lines))
    wanted, sub_x, sub_y, cosine, sine, thrust = [per_slot(values) for values in shifted]
    own = (
        me * turb_dev + lax.broadcasted_iota(jnp.int32, (turb_dev, LANES), 0)
    ).astype(jnp.float32)
    targets = jnp.concatenate([own, jnp.broadcast_to(wanted, (RECV, LANES))], axis=0)

    def collect(d, carry):
        sum_x, sum_y = carry
        for group in range(groups):
            hit = targets == table[d, pl.ds(5 + group, 1)]
            sum_x = sum_x + jnp.where(hit, every[d, pl.ds(group, 1)], 0.0)
            sum_y = sum_y + jnp.where(hit, every[d, pl.ds(groups + group, 1)], 0.0)
        return sum_x, sum_y

    zero = jnp.zeros((turb_dev + RECV, LANES), jnp.float32)
    sums = lax.fori_loop(0, n, collect, (zero, zero), unroll=2)
    step = step_size[0]
    taken = [
        jnp.clip(-step * jnp.sum(part, axis=1, keepdims=True), -0.5, 0.5) for part in sums
    ]
    flip = lax.broadcasted_iota(jnp.int32, (turb_dev, turb_dev), 0) == lax.broadcasted_iota(
        jnp.int32, (turb_dev, turb_dev), 1
    )
    for i in range(2):
        step_out[i : i + 1] = jnp.sum(
            jnp.where(flip, taken[i][:turb_dev], 0.0), axis=0, keepdims=True
        )
    cells = KX * KY * KZ
    cell = lax.broadcasted_iota(jnp.int32, (RECV, cells), 1)
    ex = (cell // (KY * KZ)).astype(jnp.float32) + 0.5 - KX / 2.0
    ey = lax.rem(cell // KZ, KY).astype(jnp.float32) + 0.5 - KY / 2.0
    ez = lax.rem(cell, KZ).astype(jnp.float32) + 0.5 - KZ / 2.0
    delta_x = ex - (sub_x + taken[0][turb_dev:])
    delta_y = ey - (sub_y + taken[1][turb_dev:])
    along = cosine * delta_x + sine * delta_y
    across = cosine * delta_y - sine * delta_x
    kernel = thrust * jnp.exp(
        -along * along / (2.0 * SIGMA_AXIAL * SIGMA_AXIAL)
        - (across * across + ez * ez) / (2.0 * SIGMA_RADIAL * SIGMA_RADIAL)
    )
    incoming[...] = jnp.where(valid > 0, kernel, 0.0).astype(jnp.bfloat16)


def finish(step_size, slopes, table, turb_dev, groups, moved_dev, sizes):
    n = sizes[0] * sizes[1]
    vmem = pl.BlockSpec(memory_space=pltpu.VMEM)

    every = pl.pallas_call(
        functools.partial(share_kernel, sizes),
        out_shape=jax.ShapeDtypeStruct((n,) + slopes.shape, jnp.float32),
        in_specs=[vmem],
        out_specs=vmem,
        scratch_shapes=[
            pltpu.VMEM((n,) + slopes.shape, jnp.float32),
            pltpu.SemaphoreType.DMA((sizes[0] + sizes[1],)),
            pltpu.SemaphoreType.DMA((sizes[0] + sizes[1],)),
        ],
        compiler_params=pltpu.CompilerParams(collective_id=1, has_side_effects=True),
        name="share",
    )(slopes)
    return pl.pallas_call(
        functools.partial(finish_kernel, sizes, groups, moved_dev),
        out_shape=(
            jax.ShapeDtypeStruct((2, turb_dev), jnp.float32),
            jax.ShapeDtypeStruct((RECV, KX * KY * KZ), jnp.bfloat16),
        ),
        in_specs=[pl.BlockSpec(memory_space=pltpu.SMEM), vmem, vmem],
        out_specs=(vmem, vmem),
        name="finish",
    )(step_size, every, table)


def body(
    sizes, adjoint, medium, rotors, step_size, slot_turbine, slot_corner, moved_rotors, new_brick
):
    turb_dev = rotors.shape[1]
    groups = -(-slot_turbine.shape[0] // LANES)
    state, table = relax(adjoint, medium, rotors, slot_turbine, moved_rotors, new_brick, sizes)
    state, slopes = slot_slopes(state, slot_turbine, slot_corner, table, turb_dev)
    step_taken, incoming = finish(
        step_size.reshape(1), slopes, table, turb_dev, groups, moved_rotors.shape[0], sizes
    )
    return (state, step_taken, incoming)


def solution(mesh):
    sizes = (mesh.shape["gx"], mesh.shape["gy"])
    return jax.shard_map(
        functools.partial(body, sizes),
        mesh=mesh,
        in_specs=(
            P(None, "gx", "gy", None),
            P(None, "gx", "gy", None),
            P(None, ("gx", "gy")),
            P(),
            P(("gx", "gy")),
            P(None, ("gx", "gy")),
            P(("gx", "gy")),
            P(("gx", "gy"), None),
        ),
        out_specs=(P(None, "gx", "gy", None), P(None, ("gx", "gy")), P(("gx", "gy"), None)),
        check_vma=False,
    )
```
